32 devices in a mesh: blk: 32 (over z, y, x, core).
Axes of the slice: x: 2, y: 2, z: 4, core: 2. Of those that a mesh axis runs over, the one named last changes fastest.
Arguments:
- populations: float32 [128, 27, 4096], P('blk'), may hold values from 0.6 to 1.4
- scalars: float32 [128, 9, 4096], P('blk'), may hold values from 0 to 1
- coarse_old: float32 [128, 27, 512], P('blk'), may hold values from 0.6 to 1.4
- coarse_new: float32 [128, 27, 512], P('blk'), may hold values from 0.6 to 1.4
- levels: int32 [128], replicated, may hold values 0 or 1
- neighbours: int32 [128, 6], P('blk'), may hold values from 0 to 127, as said below
- relax_rates: float32 [27], replicated, may hold values from 0.5 to 1.9
- diffusivity: float32 [9], replicated, may hold values from 0.02 to 0.15
- stoichiometry: float32 [9], replicated, may hold values from -1 to 1
Outputs:
- new_populations: float32 [128, 27, 4096], P('blk')
- new_scalars: float32 [128, 9, 4096], P('blk')
- coarse_return: float32 [128, 3456], P('blk')
The draws below stay inside these ranges and needn't reach their ends.
Inputs may be any that keep to these rules, and one draw needn't show every extreme that they name: `neighbours`: block k lies in slot k % 4 of device k // 4. The blocks 4 * 2 * L up to 4 * 2 * (L + 1) - 1 form layer L (0 <= L < 16), held by devices 2 L and 2 L + 1; the blocks beside a block of layer L on sides 0 to 3 lie in layer L, the one on side 4 in layer L - 1 and the one on side 5 in layer L + 1, taken modulo 16. The relation is symmetric: if m is beside k on side q, k is beside m on side q xor 1. Hence the device of every listed block is at most 3 devices from the device of block k, counting cyclically over all devices.
All inputs are finite; a program needn't handle non-finite values.
Results may differ from the reference program's by a relative error of at most 0.0001.
Values sent between devices are 32-bit elements; how exact they have to be, the bound alone decides.
A program may use at most 128 MiB of HBM per device.

```python
import math
import jax
import jax.numpy as jnp
import numpy as np
from jax import lax

BLOCK_EDGE = 16
HALF_EDGE = 8
VELOCITIES = 27
SCALARS = 9
LAYER_X = 4
LAYER_Y = 2
LAYERS = 16
BLOCKS = 128


def layer_order(layer_key):
    return jax.random.permutation(layer_key, LAYER_X * LAYER_Y)


def draw_neighbours(key, part):
    per_layer = LAYER_X * LAYER_Y
    layer_keys = jax.random.split(jax.random.fold_in(key, 17), LAYERS)
    placed = jax.vmap(layer_order)(layer_keys).astype(jnp.int32)
    inverse_place = jnp.argsort(placed, axis=1).astype(jnp.int32)
    numbers = jnp.arange(BLOCKS, dtype=jnp.int32)
    layer_index = numbers // per_layer
    position = placed[layer_index, numbers % per_layer]
    column_x = position % LAYER_X
    column_y = position // LAYER_X

    def number_at(layer_at, x_at, y_at):
        wrapped = layer_at % LAYERS
        return wrapped * per_layer + inverse_place[wrapped, y_at % LAYER_Y * LAYER_X + x_at % LAYER_X]
    columns = [number_at(layer_index, column_x - 1, column_y), number_at(layer_index, column_x + 1, column_y), number_at(layer_index, column_x, column_y - 1), number_at(layer_index, column_x, column_y + 1), number_at(layer_index - 1, column_x, column_y), number_at(layer_index + 1, column_x, column_y)]
    return jnp.stack(columns, axis=1).astype(jnp.int32)


def touch_ends(values, stream_key, least, largest):
    longest = values.shape.index(max(values.shape))
    spots = []
    for shift in (0, 1):
        where = [jax.random.randint(jax.random.fold_in(stream_key, axis), (), 0, length) for axis, length in enumerate(values.shape)]
        where[longest] = (where[longest] + shift) % values.shape[longest]
        spots.append(tuple(where))
    return values.at[spots[0]].set(least).at[spots[1]].set(largest)


def block_scale(stream_key, dims, shards, least, top_value):
    factor_of = 1.0
    for dim, parts in shards:
        heights = jax.random.uniform(jax.random.fold_in(jax.random.fold_in(stream_key, 6), dim), (parts,), jnp.float32, least / len(shards), top_value / len(shards))
        factor_of = factor_of * jnp.repeat(jnp.exp(heights), dims[dim] // parts).reshape((-1,) + (1,) * (len(dims) - 1 - dim))
    return factor_of


def setup_inputs(seed: int = 0) -> dict:
    key_list = jax.random.split(jax.random.key(seed), 10)
    return {
        "populations": jnp.clip(0.6 + 0.79999995 * jax.random.uniform(key_list[0], (BLOCKS, VELOCITIES, BLOCK_EDGE ** 3), jnp.float32) ** block_scale(key_list[0], (BLOCKS, VELOCITIES, BLOCK_EDGE ** 3), ((0, 32),), -0.2, 0.2), 0.6, 1.4),
        "scalars": jnp.clip(1.0 * jax.random.uniform(key_list[1], (BLOCKS, SCALARS, BLOCK_EDGE ** 3), jnp.float32) ** block_scale(key_list[1], (BLOCKS, SCALARS, BLOCK_EDGE ** 3), ((0, 32),), -0.2, 0.2), 0.0, 1.0),
        "coarse_old": jnp.clip(0.6 + 0.79999995 * jax.random.uniform(key_list[2], (BLOCKS, VELOCITIES, HALF_EDGE ** 3), jnp.float32) ** block_scale(key_list[2], (BLOCKS, VELOCITIES, HALF_EDGE ** 3), ((0, 32),), -0.2, 0.2), 0.6, 1.4),
        "coarse_new": jnp.clip(0.6 + 0.79999995 * jax.random.uniform(key_list[3], (BLOCKS, VELOCITIES, HALF_EDGE ** 3), jnp.float32) ** block_scale(key_list[3], (BLOCKS, VELOCITIES, HALF_EDGE ** 3), ((0, 32),), -0.2, 0.2), 0.6, 1.4),
        "levels": touch_ends((jax.random.randint(key_list[4], (BLOCKS,), 0, 5) < 3).astype(jnp.int32), jax.random.fold_in(key_list[4], 1), 0, 1),
        "neighbours": draw_neighbours(jax.random.fold_in(key_list[9], 71), 0),
        "relax_rates": jnp.clip(jnp.exp(jax.random.uniform(key_list[6], (VELOCITIES,), jnp.float32, math.log(0.5), math.log(1.9))), 0.5, 1.9),
        "diffusivity": jnp.clip(jnp.exp(jax.random.uniform(key_list[7], (SCALARS,), jnp.float32, math.log(0.02), math.log(0.15))), 0.02, 0.15),
        "stoichiometry": jnp.clip(jax.random.uniform(key_list[8], (SCALARS,), jnp.float32, -1.0, 1.0), -1.0, 1.0),
    }


PREFACTOR = 1.0
ZELDOVICH = 4.0


def lattice_tables():
    steps_one = (-1.0, 0.0, 1.0)
    velocities = np.array([[a, b, c] for a in steps_one for b in steps_one for c in steps_one])
    weights = np.prod(np.where(velocities == 0, 2.0 / 3.0, 1.0 / 6.0), axis=1)
    vander = np.array([[1.0, 1.0, 1.0], [-1.0, 0.0, 1.0], [1.0, 0.0, 1.0]])
    moments = np.kron(np.kron(vander, vander), vander)
    inverse = np.array([[0.0, -0.5, 0.5], [1.0, 0.0, -1.0], [0.0, 0.5, 0.5]])
    inverse_moments = np.kron(np.kron(inverse, inverse), inverse)
    return velocities, weights, moments, inverse_moments


def relaxation(relax_rates):
    velocities, weights, moments, inverse_moments = lattice_tables()
    left_part = jnp.asarray(inverse_moments / weights[:, None], jnp.float32)
    right_part = jnp.asarray(moments * weights[None, :], jnp.float32)
    return jnp.dot(left_part * relax_rates[None, :], right_part, precision=lax.Precision.HIGHEST, preferred_element_type=jnp.float32)


def moment_rows():
    velocities, weights, moments, inverse_moments = lattice_tables()
    return np.concatenate([weights[None, :], (velocities * weights[:, None]).T], axis=0)


def cell_stride(direction, extent):
    return extent ** (2 - direction)


def coordinate_of(direction, extent):
    return jnp.asarray((np.arange(extent ** 3) // cell_stride(direction, extent)) % extent, jnp.int32)


def layer_of(flat, direction, upward, extent):
    index = (extent - 1) * upward
    last_axis = flat.ndim - 1
    lead = flat.shape[:-1]
    if direction == 0:
        return lax.slice_in_dim(flat, index * extent * extent, (index + 1) * extent * extent, axis=last_axis)
    if direction == 1:
        shaped = flat.reshape(lead + (extent, extent * extent))
        picked = lax.slice_in_dim(shaped, index * extent, (index + 1) * extent, axis=last_axis + 1)
        return picked.reshape(lead + (extent * extent,))
    return lax.slice_in_dim(flat, index, flat.shape[-1], stride=extent, axis=last_axis)


def spread_face(face, direction, extent):
    lead = face.shape[:-1]
    if direction == 0:
        return jnp.tile(face, (1,) * len(lead) + (extent,))
    if direction == 1:
        square_face = face.reshape(lead + (extent, extent))
        tiled = jnp.tile(square_face, (1,) * (len(lead) + 1) + (extent,))
        return tiled.reshape(lead + (extent ** 3,))
    return jnp.repeat(face, extent, axis=len(lead))


def move_up(flat, face, direction, extent):
    stride = cell_stride(direction, extent)
    lead = flat.shape[:-1]
    shifted = jnp.concatenate([jnp.zeros(lead + (stride,), flat.dtype), flat[..., :-stride]], axis=len(lead))
    return jnp.where(coordinate_of(direction, extent) == 0, spread_face(face, direction, extent), shifted)


def move_down(flat, face, direction, extent):
    stride = cell_stride(direction, extent)
    lead = flat.shape[:-1]
    shifted = jnp.concatenate([flat[..., stride:], jnp.zeros(lead + (stride,), flat.dtype)], axis=len(lead))
    return jnp.where(coordinate_of(direction, extent) == extent - 1, spread_face(face, direction, extent), shifted)


def collide(lattice_state, operator_matrix):
    blocks = lattice_state.shape[0]
    velocities, weights, moments, inverse_moments = lattice_tables()
    flattened = lattice_state.reshape(blocks, 27, -1)
    moment_sums = jnp.einsum('pi,bic->bpc', jnp.asarray(moment_rows(), jnp.float32), flattened, precision=lax.Precision.HIGHEST)
    density = moment_sums[:, 0:1]
    current = moment_sums[:, 1:4]
    projected = jnp.einsum('id,bdc->bic', jnp.asarray(velocities, jnp.float32), current, precision=lax.Precision.HIGHEST)
    square = jnp.sum(current * current, axis=1, keepdims=True)
    balance = density + 3.0 * projected + 4.5 * projected * projected - 1.5 * square
    relaxed = flattened - jnp.einsum('ik,bkc->bic', operator_matrix, flattened - balance, precision=lax.Precision.HIGHEST)
    return relaxed.reshape(lattice_state.shape)


def outgoing(relaxed, extent):
    blocks = relaxed.shape[0]
    halved = extent // 2
    face_list = []
    for facing in range(6):
        direction = facing // 2
        upward = facing % 2
        moving = lax.index_in_dim(relaxed, 2 * upward, 1 + direction, keepdims=False).reshape(blocks, 9, -1)
        layer_face = layer_of(moving, direction, upward, extent)
        grouped = layer_face.reshape(blocks, 9, halved, 2, halved, 2)
        merged = jnp.sum(grouped, axis=(3, 5)) * 0.25
        face_list.append(merged.reshape(blocks, 9, halved * halved))
    return jnp.stack(face_list, axis=1)


def enlarge(face_values, halved):
    blocks = face_values.shape[0]
    square_face = face_values.reshape(blocks, 9, halved, halved)
    grown = jnp.repeat(jnp.repeat(square_face, 2, axis=2), 2, axis=3)
    return grown.reshape(blocks, 9, 4 * halved * halved)


def crossing_faces(read, coarse_now, fine_mask, direction, extent, halved):
    blocks = read.shape[0]
    high_face = layer_of(lax.index_in_dim(read, 2, 1 + direction, False).reshape(blocks, 9, -1), direction, 1, extent)
    low_face = layer_of(lax.index_in_dim(read, 0, 1 + direction, False).reshape(blocks, 9, -1), direction, 0, extent)
    coarse_high = enlarge(layer_of(lax.index_in_dim(coarse_now, 2, 1 + direction, False).reshape(blocks, 9, -1), direction, 1, halved), halved)
    coarse_low = enlarge(layer_of(lax.index_in_dim(coarse_now, 0, 1 + direction, False).reshape(blocks, 9, -1), direction, 0, halved), halved)
    keep_fine = fine_mask[:, None, None]
    high_face = jnp.where(keep_fine, high_face, coarse_high)
    low_face = jnp.where(keep_fine, low_face, coarse_low)
    return jnp.stack([high_face, low_face], axis=1)


def apply_section(read, from_low, from_high, direction, extent):
    forward = lax.index_in_dim(read, 2, 1 + direction, False)
    backward = lax.index_in_dim(read, 0, 1 + direction, False)
    middle = lax.index_in_dim(read, 1, 1 + direction, False)
    forward = move_up(forward, from_low, direction, extent)
    backward = move_down(backward, from_high, direction, extent)
    return jnp.stack([backward, middle, forward], axis=1 + direction)


def species_rims(species, extent):
    rim_list = []
    for facing in range(6):
        rim_list.append(layer_of(species, facing // 2, facing % 2, extent))
    return jnp.stack(rim_list, axis=1)


def advance_species(species, read, halo_faces, diffusivity, stoichiometry, extent):
    blocks = species.shape[0]
    flattened = read.reshape(blocks, 27, -1)
    current = jnp.einsum('pi,bic->bpc', jnp.asarray(moment_rows()[1:4], jnp.float32), flattened, precision=lax.Precision.HIGHEST)
    drift_term = jnp.zeros_like(species)
    spread = jnp.zeros_like(species)
    for direction in range(3):
        upper_cells = move_down(species, halo_faces[:, 2 * direction + 1], direction, extent)
        lower_cells = move_up(species, halo_faces[:, 2 * direction], direction, extent)
        drift_term = drift_term + current[:, direction][:, None] * (upper_cells - lower_cells) * 0.5
        spread = spread + (upper_cells + lower_cells - 2.0 * species)
    burning = PREFACTOR * species[:, 0] * species[:, 1] * jnp.exp(ZELDOVICH * (species[:, 8] - 1.0))
    return species - drift_term + diffusivity[None, :, None] * spread + stoichiometry[None, :, None] * burning[:, None]


def reference(populations, scalars, coarse_old, coarse_new, levels, neighbours, relax_rates, diffusivity, stoichiometry):
    blocks = populations.shape[0]
    extent = BLOCK_EDGE
    halved = HALF_EDGE
    operator_matrix = relaxation(relax_rates)
    fine_mask = levels == 1
    neighbour_fine = fine_mask[neighbours]
    lattice_state = populations.reshape(blocks, 3, 3, 3, -1)
    species = scalars
    old_coarse = coarse_old.reshape(blocks, 3, 3, 3, -1)
    new_coarse = coarse_new.reshape(blocks, 3, 3, 3, -1)
    returned = jnp.zeros((blocks, 6, 9, halved * halved), jnp.float32)
    for substep in range(2):
        coarse_now = old_coarse if substep == 0 else 0.5 * (old_coarse + new_coarse)
        relaxed = collide(lattice_state, operator_matrix)
        returned = returned + 0.5 * jnp.where(fine_mask[:, None, None, None], outgoing(relaxed, extent), 0.0)
        read = relaxed
        for direction in range(3):
            face_table = crossing_faces(read, coarse_now, fine_mask, direction, extent, halved)
            from_low = face_table[neighbours[:, 2 * direction], 0].reshape(blocks, 3, 3, extent * extent)
            from_high = face_table[neighbours[:, 2 * direction + 1], 1].reshape(blocks, 3, 3, extent * extent)
            read = apply_section(read, from_low, from_high, direction, extent)
        rim_faces = species_rims(species, extent)
        halo_list = []
        for facing in range(6):
            received = rim_faces[neighbours[:, facing], facing ^ 1]
            halo_list.append(jnp.where(neighbour_fine[:, facing][:, None, None], received, rim_faces[:, facing]))
        species = advance_species(species, read, jnp.stack(halo_list, axis=1), diffusivity, stoichiometry, extent)
        lattice_state = read
    coarse_list = [returned[neighbours[:, facing], facing ^ 1] for facing in range(6)]
    coarse_return = jnp.where(fine_mask[:, None, None, None], 0.0, jnp.stack(coarse_list, axis=1)).reshape(blocks, -1)
    new_populations = jnp.where(fine_mask[:, None, None], lattice_state.reshape(populations.shape), populations)
    new_scalars = jnp.where(fine_mask[:, None, None], species, scalars)
    return new_populations, new_scalars, coarse_return
```

```python
import jax
import jax.numpy as jnp
import numpy as np
from jax import lax
from jax.experimental import pallas as pl
from jax.experimental.pallas import tpu as pltpu
from jax.sharding import PartitionSpec as P

F32 = jnp.float32
MESH = pl.DeviceIdType.MESH
LANES = 128
ROWS = 32
HALF = 16
MOVERS = (
    (tuple(18 + p for p in range(9)), tuple(p for p in range(9))),
    (
        tuple(9 * (p // 3) + 6 + p % 3 for p in range(9)),
        tuple(9 * (p // 3) + p % 3 for p in range(9)),
    ),
    (tuple(3 * p + 2 for p in range(9)), tuple(3 * p for p in range(9))),
)
SCALAR_ROWS = (tuple(range(9)), tuple(range(9)))
XR = 40
POP_ROWS = 36 * 32
SCA_ROWS = 20 * 32
YR = 48


def lanes_of(rows):
    return lax.broadcasted_iota(jnp.int32, (rows, LANES), 1)


def flag(value, rows):
    return jnp.broadcast_to(value, (rows, LANES)) == 1


def roll(v, by, axis=1):
    size = v.shape[axis]
    by = by % size
    return v if by == 0 else pltpu.roll(v, by, axis)


def along(values, dim, func):
    out = [None] * 27
    step = (9, 3, 1)[dim]
    for base in range(27):
        if (base // step) % 3 == 0:
            a, b, c = func(values[base], values[base + step], values[base + 2 * step])
            out[base], out[base + step], out[base + 2 * step] = a, b, c
    return out


def to_moments(low, mid, high):
    both = low + high
    return both + 4.0 * mid, high - low, both


def from_moments(m0, m1, m2):
    return m2 - m1, m0 - 0.5 * m2, m1 + m2


def pack_x(load, put):
    for way in range(2):
        for half in range(2):
            put(way * 18 + half * 9, 9, load(0, way, None, half * HALF + (15 if way == 0 else 0)))


def pack_y(load, put):
    lane = lanes_of(HALF)
    last = None
    for way in range(2):
        slab = None
        for p in range(9):
            v = load(1, way, p, HALF if way == 0 else 0, HALF)
            source = 7 if way == 0 else 0
            slot = p if p < 8 else way
            v = roll(v, 16 * (slot - source))
            if p < 8:
                slab = v if slab is None else jnp.where(lane // 16 == slot, v, slab)
            else:
                last = v if last is None else jnp.where(lane // 16 == slot, v, last)
        put(way * HALF, HALF, slab)
    put(2 * HALF, HALF, last)


def pack_z(load, put):
    lane = lanes_of(ROWS) % 16
    for way in range(2):
        slab = None
        for p in range(9):
            v = roll(load(2, way, p, 0, ROWS), p - (15 if way == 0 else 0))
            slab = v if slab is None else jnp.where(lane == p, v, slab)
        put(way, slab)


def slab_face(ref, at, way, p, start):
    if p < 8:
        return roll(ref[at, pl.ds(way * HALF, HALF), :], start - 16 * p)
    return roll(ref[at, pl.ds(2 * HALF, HALF), :], start - 16 * way)


def kernel(
    levels,
    neighbours,
    rates,
    diffusivity,
    stoichiometry,
    pop,
    sca,
    old,
    new,
    out_pop,
    out_sca,
    ret_x,
    ret_y,
    ret_z,
    state,
    first,
    up0,
    up1,
    spec,
    spec2,
    lhs,
    res,
    bx_0,
    bx_1,
    by_0,
    by_1,
    bz_out_0,
    bz_out_1,
    bz_0,
    bz_1,
    sxy_0,
    sxy_1,
    sz_out_0,
    sz_out_1,
    sz_0,
    sz_1,
    rxy,
    rz_out,
    rz,
    send_sem,
    recv_sem,
):
    slots = pop.shape[0]
    devices = lax.axis_size("blk")
    me = lax.axis_index("blk")
    layers = devices // 2
    layer = me // 2
    core = me % 2
    partner = 2 * layer + 1 - core
    above = lax.rem(layer + 1, layers)
    below = lax.rem(layer + layers - 1, layers)
    mine = core * slots
    around = 2 * slots
    mesh_targets = ((2 * above, 2 * above + 1), (2 * below, 2 * below + 1))

    barrier = pltpu.get_barrier_semaphore()
    for device in (partner,) + mesh_targets[0] + mesh_targets[1]:
        pl.semaphore_signal(barrier, inc=1, device_id=(device,), device_id_type=MESH)

    counter = [0, 0]

    def send_partner(ref):
        s, r = counter[0], counter[1]
        counter[0] += 1
        counter[1] += 1
        part = ref.at[pl.ds(mine, slots)]
        copy = pltpu.make_async_remote_copy(
            src_ref=part,
            dst_ref=part,
            send_sem=send_sem.at[s],
            recv_sem=recv_sem.at[r],
            device_id=(partner,),
            device_id_type=MESH,
        )
        copy.start()
        other = ref.at[pl.ds(slots - mine, slots)]
        arrival = pltpu.make_async_remote_copy(
            src_ref=other,
            dst_ref=other,
            send_sem=send_sem.at[s],
            recv_sem=recv_sem.at[r],
            device_id=(partner,),
            device_id_type=MESH,
        )

        def wait():
            arrival.wait_recv()
            copy.wait_send()

        return wait

    def send_layers(source, target):
        waits = []
        for way in range(2):
            r = counter[1]
            counter[1] += 2
            for core_to in range(2):
                s = counter[0]
                counter[0] += 1
                copy = pltpu.make_async_remote_copy(
                    src_ref=source.at[way],
                    dst_ref=target.at[way, pl.ds(mine, slots)],
                    send_sem=send_sem.at[s],
                    recv_sem=recv_sem.at[r + core],
                    device_id=(mesh_targets[way][core_to],),
                    device_id_type=MESH,
                )
                copy.start()
                waits.append(copy.wait_send)
                arrival = pltpu.make_async_remote_copy(
                    src_ref=source.at[way],
                    dst_ref=target.at[way, pl.ds(core_to * slots, slots)],
                    send_sem=send_sem.at[s],
                    recv_sem=recv_sem.at[r + core_to],
                    device_id=(mesh_targets[way][core_to],),
                    device_id_type=MESH,
                )
                waits.append(arrival.wait_recv)

        def wait():
            for w in waits:
                w()

        return wait

    def each_block(body):
        def wrapped(b, carry):
            body(b)
            return carry

        lax.fori_loop(0, slots, wrapped, 0)

    def fine_of(b):
        return levels[me * slots + b]

    def place(b, q):
        return lax.rem(neighbours[b, q], around)

    def unpack_in(b):
        def one(x, carry):
            for half in range(2):
                column = pl.ds(pl.multiple_of((2 * x + half) * LANES, LANES), LANES)
                row = half * HALF + x
                state[b, pl.ds(row, 27, stride=ROWS), :] = pop[b, :, column]
                spec[b, pl.ds(row, 9, stride=ROWS), :] = sca[b, :, column]
            return carry

        lax.fori_loop(0, HALF, one, 0)

    each_block(unpack_in)

    def spread_coarse(target, average):
        lhs[...] = jnp.zeros(lhs.shape, F32)
        for b in range(slots):
            for chunk in range(4):
                v = old[b, :, pl.ds(chunk * LANES, LANES)]
                if average:
                    v = 0.5 * (v + new[b, :, pl.ds(chunk * LANES, LANES)])
                lhs[pl.ds((b * 4 + chunk) * ROWS, 27), :] = v
        a = lhs[...]
        a0 = a.astype(jnp.bfloat16)
        rest = a - a0.astype(F32)
        a1 = rest.astype(jnp.bfloat16)
        a2 = (rest - a1.astype(F32)).astype(jnp.bfloat16)
        row = lax.broadcasted_iota(jnp.int32, (LANES, LANES), 0)
        col = lax.broadcasted_iota(jnp.int32, (LANES, LANES), 1)
        want = (col // 32) * 8 + (col % 16) // 2
        for variant in range(4):
            parity, half = variant // 2, variant % 2
            pick = jnp.where(row == want + parity * 64 + half * 32, 1.0, 0.0).astype(jnp.bfloat16)
            total = jnp.dot(a0, pick, preferred_element_type=F32)
            total = total + jnp.dot(a1, pick, preferred_element_type=F32)
            total = total + jnp.dot(a2, pick, preferred_element_type=F32)
            res[...] = total

            def scatter(g, carry):
                v = res[pl.ds(pl.multiple_of(g * ROWS, ROWS), 27), :]
                b = g // 4
                x = 2 * (2 * (g % 4) + parity)
                target[b, pl.ds(half * HALF + x, 27, stride=ROWS), :] = v
                target[b, pl.ds(half * HALF + x + 1, 27, stride=ROWS), :] = v
                return carry

            lax.fori_loop(0, slots * 4, scatter, 0)

    spread_coarse(up0, False)
    spread_coarse(up1, True)

    def population_load(b, spread):
        fine = fine_of(b)

        def load(dim, way, p, start, size=None):
            movers = MOVERS[dim][way]
            if p is None:
                at = pl.ds(ROWS * movers[0] + start, 9, stride=ROWS)
                return jnp.where(flag(fine, 9), state[b, at, :], spread[b, at, :])
            at = pl.ds(ROWS * movers[p] + start, size)
            return jnp.where(flag(fine, size), state[b, at, :], spread[b, at, :])

        return load

    def return_load(b):
        fine = fine_of(b)

        def load(dim, way, p, start, size=None):
            movers = MOVERS[dim][way]
            if p is None:
                at = pl.ds(ROWS * movers[0] + start, 9, stride=ROWS)
                rows = 9
            else:
                at = pl.ds(ROWS * movers[p] + start, size)
                rows = size
            return jnp.where(flag(fine, rows), 0.5 * first[b, at, :] + 0.5 * state[b, at, :], 0.0)

        return load

    def scalar_load(b, source):
        def load(dim, way, p, start, size=None):
            if p is None:
                return source[b, pl.ds(start, 9, stride=ROWS), :]
            return source[b, pl.ds(ROWS * p + start, size), :]

        return load

    def putter(ref, at, base=0):
        def put(start, size, value):
            ref[at, pl.ds(base + start, size), :] = value

        return put

    def putter_z(ref, b):
        def put(way, value):
            ref[way, b] = value

        return put

    def collide(keep):
        scale = [rates[k] * (3.375 / 216.0 * 2.0 ** sum(1 for d in (9, 3, 1) if (k // d) % 3)) for k in range(27)]

        def one(t, carry):
            b = t // 4
            base = pl.multiple_of((t % 4) * 8, 8)

            def at(i):
                return pl.ds(base + ROWS * i, 8)

            g = [state[b, at(i), :] for i in range(27)]
            m = along(along(along(g, 2, to_moments), 1, to_moments), 0, to_moments)
            rho = m[0]
            jx, jy, jz = m[9], m[3], m[1]
            unit = 1.0 / 216.0
            hx, hy, hz = jx * unit, jy * unit, jz * unit
            third = 1.0 / 3.0
            qx, qy, qz = jx * hx, jy * hy, jz * hz
            eq = [None] * 27
            eq[0] = rho
            eq[9], eq[3], eq[1] = jx, jy, jz
            rho3 = rho * third
            eq[18], eq[6], eq[2] = rho3 + qx, rho3 + qy, rho3 + qz
            xy, xz, yz = jx * hy, jx * hz, jy * hz
            eq[12], eq[10], eq[4] = xy, xz, yz
            jx3, jy3, jz3 = jx * third, jy * third, jz * third
            eq[21], eq[19] = jy3, jz3
            eq[15], eq[7] = jx3, jz3
            eq[11], eq[5] = jx3, jy3
            rho9 = rho3 * third
            qx3, qy3, qz3 = qx * third, qy * third, qz * third
            eq[24] = rho9 + qx3 + qy3
            eq[20] = rho9 + qx3 + qz3
            eq[8] = rho9 + qy3 + qz3
            eq[22], eq[16], eq[14] = yz * third, xz * third, xy * third
            eq[25], eq[23], eq[17] = jz3 * third, jy3 * third, jx3 * third
            eq[26] = (rho9 + qx3 + qy3 + qz3) * third
            delta = [
                scale[k] * (m[k] if eq[k] is None else m[k] - eq[k]) for k in range(27)
            ]
            back = along(along(along(delta, 0, from_moments), 1, from_moments), 2, from_moments)
            for i in range(27):
                post = state[b, at(i), :] - back[i]
                state[b, at(i), :] = post
                if keep:
                    first[b, at(i), :] = post
            return carry

        lax.fori_loop(0, slots * 4, one, 0)

    def section_x(recv):
        def body(b):
            for p in range(9):
                for half in range(2):
                    up = ROWS * MOVERS[0][0][p] + half * HALF
                    down = ROWS * MOVERS[0][1][p] + half * HALF
                    v = state[b, pl.ds(up, 15), :]
                    w = state[b, pl.ds(down + 1, 15), :]
                    state[b, pl.ds(up + 1, 15), :] = v
                    state[b, pl.ds(down, 15), :] = w
            low, high = place(b, 0), place(b, 1)
            for half in range(2):
                state[b, pl.ds(ROWS * 18 + half * HALF, 9, stride=ROWS), :] = recv[
                    low, pl.ds(half * 9, 9), :
                ]
                state[b, pl.ds(half * HALF + 15, 9, stride=ROWS), :] = recv[
                    high, pl.ds(18 + half * 9, 9), :
                ]

        each_block(body)

    def section_y(recv):
        def body(b):
            lane = lanes_of(HALF)
            low, high = place(b, 2), place(b, 3)
            for p in range(9):
                i = MOVERS[1][0][p]
                e = roll(state[b, pl.ds(ROWS * i, HALF), :], 16)
                o = roll(state[b, pl.ds(ROWS * i + HALF, HALF), :], 16)
                state[b, pl.ds(ROWS * i + HALF, HALF), :] = jnp.where(lane < 16, e, o)
                state[b, pl.ds(ROWS * i, HALF), :] = jnp.where(
                    lane < 16, slab_face(recv, low, 0, p, 0), e
                )
                i = MOVERS[1][1][p]
                e = roll(state[b, pl.ds(ROWS * i, HALF), :], -16)
                o = roll(state[b, pl.ds(ROWS * i + HALF, HALF), :], -16)
                state[b, pl.ds(ROWS * i, HALF), :] = jnp.where(lane >= 112, o, e)
                state[b, pl.ds(ROWS * i + HALF, HALF), :] = jnp.where(
                    lane >= 112, slab_face(recv, high, 1, p, 112), o
                )

        each_block(body)

    def section_z(recv):
        def body(b):
            lane = lanes_of(ROWS) % 16
            low = recv[0, place(b, 4)]
            high = recv[1, place(b, 5)]
            for p in range(9):
                at = pl.ds(ROWS * MOVERS[2][0][p], ROWS)
                state[b, at, :] = jnp.where(lane == 0, roll(low, -p), roll(state[b, at, :], 1))
                at = pl.ds(ROWS * MOVERS[2][1][p], ROWS)
                state[b, at, :] = jnp.where(
                    lane == 15, roll(high, 15 - p), roll(state[b, at, :], -1)
                )

        each_block(body)

    def advance(source, target, recv, recv_z):
        def body(b):
            row = lax.broadcasted_iota(jnp.int32, (HALF, LANES), 0)
            lane = lanes_of(HALF)
            near = lane % 16
            known = [flag(levels[neighbours[b, q]], HALF) for q in range(6)]
            spot = [place(b, q) for q in range(6)]
            e8 = [source[b, pl.ds(ROWS * 8 + h * HALF, HALF), :] for h in range(2)]
            burn = [
                source[b, pl.ds(h * HALF, HALF), :]
                * source[b, pl.ds(ROWS + h * HALF, HALF), :]
                * jnp.exp(4.0 * (e8[h] - 1.0))
                for h in range(2)
            ]
            drift = []
            for half in range(2):

                def get(i):
                    return state[b, pl.ds(ROWS * i + half * HALF, HALF), :]

                g = [get(i) for i in range(27)]
                weighted = lambda a, c, f: (a + f) * (1.0 / 6.0) + c * (2.0 / 3.0)
                slope = lambda a, f: (f - a) * (1.0 / 6.0)
                zsum = [weighted(g[3 * k], g[3 * k + 1], g[3 * k + 2]) for k in range(9)]
                zdif = [slope(g[3 * k], g[3 * k + 2]) for k in range(9)]
                ysum = [weighted(zsum[3 * k], zsum[3 * k + 1], zsum[3 * k + 2]) for k in range(3)]
                ydif = [slope(zsum[3 * k], zsum[3 * k + 2]) for k in range(3)]
                zrow = [weighted(zdif[3 * k], zdif[3 * k + 1], zdif[3 * k + 2]) for k in range(3)]
                drift.append((slope(ysum[0], ysum[2]), weighted(*ydif), weighted(*zrow)))
            for m in range(9):
                e = source[b, pl.ds(ROWS * m, HALF), :]
                o = source[b, pl.ds(ROWS * m + HALF, HALF), :]
                pair = (e, o)
                up_y, down_y = roll(e, -16), roll(o, -16)
                up_y = (
                    jnp.where(lane >= 112, down_y, up_y),
                    jnp.where(
                        lane >= 112,
                        jnp.where(known[3], slab_face(recv.at[:, pl.ds(XR, YR)], spot[3], 1, m, 112), o),
                        down_y,
                    ),
                )
                re, ro = roll(e, 16), roll(o, 16)
                down_y = (
                    jnp.where(
                        lane < 16,
                        jnp.where(known[2], slab_face(recv.at[:, pl.ds(XR, YR)], spot[2], 0, m, 0), e),
                        re,
                    ),
                    jnp.where(lane < 16, re, ro),
                )
                for half in range(2):
                    v = pair[half]
                    line = recv[spot[0], pl.ds(half * 9 + m, 1), :]
                    face = jnp.where(known[0], jnp.broadcast_to(line, v.shape), v)
                    down_x = jnp.where(row == 0, face, roll(v, 1, 0))
                    line = recv[spot[1], pl.ds(18 + half * 9 + m, 1), :]
                    face = jnp.where(known[1], jnp.broadcast_to(line, v.shape), v)
                    up_x = jnp.where(row == 15, face, roll(v, -1, 0))
                    face = roll(recv_z[0, spot[4], pl.ds(half * HALF, HALF), :], -m)
                    down_z = jnp.where(near == 0, jnp.where(known[4], face, v), roll(v, 1))
                    face = roll(recv_z[1, spot[5], pl.ds(half * HALF, HALF), :], 15 - m)
                    up_z = jnp.where(near == 15, jnp.where(known[5], face, v), roll(v, -1))
                    jx, jy, jz = drift[half]
                    moved = (
                        jx * (up_x - down_x)
                        + jy * (up_y[half] - down_y[half])
                        + jz * (up_z - down_z)
                    )
                    spread = (up_x + down_x) + (up_y[half] + down_y[half]) + (up_z + down_z) - 6.0 * v
                    target[b, pl.ds(ROWS * m + half * HALF, HALF), :] = (
                        v - 0.5 * moved + diffusivity[m] * spread + stoichiometry[m] * burn[half]
                    )

        each_block(body)

    pl.semaphore_wait(barrier, 5)
    last_wait = None
    for substep in range(2):
        spread = (up0, up1)[substep]
        source, target = (spec, spec2) if substep == 0 else (spec2, spec)
        cx, cy, cz_out, cz = ((bx_0, by_0, bz_out_0, bz_0), (bx_1, by_1, bz_out_1, bz_1))[substep]
        cs, cs_out, cs_z = ((sxy_0, sz_out_0, sz_0), (sxy_1, sz_out_1, sz_1))[substep]

        def pack_scalars(b):
            load = scalar_load(b, source)
            pack_x(load, putter(cs, mine + b))
            pack_y(load, putter(cs, mine + b, XR))
            pack_z(load, putter_z(cs_out, b))

        each_block(pack_scalars)
        wait_s = send_partner(cs)
        wait_sz = send_layers(cs_out, cs_z)
        collide(substep == 0)
        each_block(lambda b: pack_x(population_load(b, spread), putter(cx, mine + b)))
        wait = send_partner(cx)
        if substep == 1:

            def pack_return(b):
                load = return_load(b)
                pack_x(load, putter(rxy, mine + b))
                pack_y(load, putter(rxy, mine + b, XR))
                pack_z(load, putter_z(rz_out, b))

            each_block(pack_return)
            wait_r = send_partner(rxy)
            wait_rz = send_layers(rz_out, rz)
        wait()
        section_x(cx)
        each_block(lambda b: pack_y(population_load(b, spread), putter(cy, mine + b)))
        send_partner(cy)()
        section_y(cy)
        each_block(lambda b: pack_z(population_load(b, spread), putter_z(cz_out, b)))
        wait = send_layers(cz_out, cz)
        wait()
        section_z(cz)
        wait_s()
        wait_sz()
        advance(source, target, cs, cs_z)
    wait_r()
    wait_rz()

    def pack_out(b):
        fine = fine_of(b)

        def one(x, carry):
            for half in range(2):
                column = pl.ds(pl.multiple_of((2 * x + half) * LANES, LANES), LANES)
                row = half * HALF + x
                out_pop[b, :, column] = jnp.where(
                    flag(fine, 27), state[b, pl.ds(row, 27, stride=ROWS), :], pop[b, :, column]
                )
                out_sca[b, :, column] = jnp.where(
                    flag(fine, 9), spec[b, pl.ds(row, 9, stride=ROWS), :], sca[b, :, column]
                )
            return carry

        lax.fori_loop(0, HALF, one, 0)
        for way in range(2):
            ret_x[b, way] = rxy[place(b, way), pl.ds(18 * way, 18), :]
            at = place(b, 2 + way)
            ret_y[b, way, pl.ds(0, HALF), :] = rxy[at, pl.ds(XR + HALF * way, HALF), :]
            ret_y[b, way, pl.ds(HALF, HALF), :] = rxy[at, pl.ds(XR + 2 * HALF, HALF), :]
            ret_z[b, way] = rz[way, place(b, 4 + way)]

    each_block(pack_out)


def local(
    populations,
    scalars,
    coarse_old,
    coarse_new,
    levels,
    neighbours,
    relax_rates,
    diffusivity,
    stoichiometry,
):
    slots = populations.shape[0]
    vmem = pl.BlockSpec(memory_space=pltpu.VMEM)
    smem = pl.BlockSpec(memory_space=pltpu.SMEM)
    shape = jax.ShapeDtypeStruct
    layer = 2 * slots
    outs = pl.pallas_call(
        kernel,
        out_shape=(
            shape(populations.shape, F32),
            shape(scalars.shape, F32),
            shape((slots, 2, 18, LANES), F32),
            shape((slots, 2, 32, LANES), F32),
            shape((slots, 2, 32, LANES), F32),
        ),
        in_specs=[smem] * 5 + [vmem] * 4,
        out_specs=[vmem] * 5,
        scratch_shapes=[
            pltpu.VMEM((slots, POP_ROWS, LANES), F32),
            pltpu.VMEM((slots, POP_ROWS, LANES), F32),
            pltpu.VMEM((slots, POP_ROWS, LANES), F32),
            pltpu.VMEM((slots, POP_ROWS, LANES), F32),
            pltpu.VMEM((slots, SCA_ROWS, LANES), F32),
            pltpu.VMEM((slots, SCA_ROWS, LANES), F32),
            pltpu.VMEM((slots * 4 * ROWS, LANES), F32),
            pltpu.VMEM((slots * 4 * ROWS, LANES), F32),
            pltpu.VMEM((layer + 1, XR, LANES), F32),
            pltpu.VMEM((layer + 1, XR, LANES), F32),
            pltpu.VMEM((layer, YR, LANES), F32),
            pltpu.VMEM((layer, YR, LANES), F32),
            pltpu.VMEM((2, slots, ROWS, LANES), F32),
            pltpu.VMEM((2, slots, ROWS, LANES), F32),
            pltpu.VMEM((2, layer, ROWS, LANES), F32),
            pltpu.VMEM((2, layer, ROWS, LANES), F32),
            pltpu.VMEM((layer, XR + YR, LANES), F32),
            pltpu.VMEM((layer, XR + YR, LANES), F32),
            pltpu.VMEM((2, slots, ROWS, LANES), F32),
            pltpu.VMEM((2, slots, ROWS, LANES), F32),
            pltpu.VMEM((2, layer, ROWS, LANES), F32),
            pltpu.VMEM((2, layer, ROWS, LANES), F32),
            pltpu.VMEM((layer, XR + YR, LANES), F32),
            pltpu.VMEM((2, slots, ROWS, LANES), F32),
            pltpu.VMEM((2, layer, ROWS, LANES), F32),
            pltpu.SemaphoreType.DMA((32,)),
            pltpu.SemaphoreType.DMA((32,)),
        ],
        compiler_params=pltpu.CompilerParams(
            collective_id=0, has_side_effects=True, vmem_limit_bytes=56 << 20
        ),
    )(
        levels,
        neighbours,
        relax_rates,
        diffusivity,
        stoichiometry,
        populations,
        scalars,
        coarse_old,
        coarse_new,
    )
    new_populations, new_scalars, ret_x, ret_y, ret_z = outs
    x = ret_x.reshape(slots, 2, 2, 9, 4, 2, 8, 2).sum(axis=(5, 7))
    x = x.transpose(0, 1, 3, 2, 4, 5).reshape(slots, 2, 9, 64)
    y = ret_y.reshape(slots, 2, 2, 8, 2, 8, 8, 2).sum(axis=(4, 7))
    y8 = jnp.stack([y[:, 0, 1, :, 0], y[:, 1, 1, :, 1]], axis=1)
    y = jnp.concatenate([y[:, :, 0], y8[:, :, :, None]], axis=3)
    y = y.transpose(0, 1, 3, 2, 4).reshape(slots, 2, 9, 64)
    z = ret_z.reshape(slots, 2, 2, 8, 2, 4, 2, 16).sum(axis=(4, 6))[..., :9]
    z = z.transpose(0, 1, 5, 3, 2, 4).reshape(slots, 2, 9, 64)
    own = lax.dynamic_slice_in_dim(levels, lax.axis_index("blk") * slots, slots)
    back = 0.25 * jnp.concatenate([x, y, z], axis=1).reshape(slots, -1)
    back = jnp.where((own == 1)[:, None], 0.0, back)
    return new_populations, new_scalars, back


def solution(mesh):
    in_specs = (
        P("blk", None, None),
        P("blk", None, None),
        P("blk", None, None),
        P("blk", None, None),
        P(),
        P("blk", None),
        P(),
        P(),
        P(),
    )
    out_specs = (P("blk", None, None), P("blk", None, None), P("blk", None))
    return jax.shard_map(local, mesh=mesh, in_specs=in_specs, out_specs=out_specs, check_vma=False)
```

```python
import jax
import jax.numpy as jnp
import numpy as np
from jax import lax
from jax.experimental import pallas as pl
from jax.experimental.pallas import tpu as pltpu
from jax.sharding import PartitionSpec as P

F32 = jnp.float32
MESH = pl.DeviceIdType.MESH
LANES = 128
ROWS = 32
HALF = 16
MOVERS = (
    (tuple(18 + p for p in range(9)), tuple(p for p in range(9))),
    (
        tuple(9 * (p // 3) + 6 + p % 3 for p in range(9)),
        tuple(9 * (p // 3) + p % 3 for p in range(9)),
    ),
    (tuple(3 * p + 2 for p in range(9)), tuple(3 * p for p in range(9))),
)
SCALAR_ROWS = (tuple(range(9)), tuple(range(9)))
XR = 40
POP_ROWS = 36 * 32
SCA_ROWS = 20 * 32
YR = 48


def lanes_of(rows):
    return lax.broadcasted_iota(jnp.int32, (rows, LANES), 1)


def flag(value, rows):
    return jnp.broadcast_to(value, (rows, LANES)) == 1


def roll(v, by, axis=1):
    size = v.shape[axis]
    by = by % size
    return v if by == 0 else pltpu.roll(v, by, axis)


def along(values, dim, func):
    out = [None] * 27
    step = (9, 3, 1)[dim]
    for base in range(27):
        if (base // step) % 3 == 0:
            a, b, c = func(values[base], values[base + step], values[base + 2 * step])
            out[base], out[base + step], out[base + 2 * step] = a, b, c
    return out


def to_moments(low, mid, high):
    both = low + high
    return both + 4.0 * mid, high - low, both


def from_moments(m0, m1, m2):
    return m2 - m1, m0 - 0.5 * m2, m1 + m2


def split(a):
    a0 = a.astype(jnp.bfloat16)
    rest = a - a0.astype(F32)
    a1 = rest.astype(jnp.bfloat16)
    return a0, a1, (rest - a1.astype(F32)).astype(jnp.bfloat16)


def product(parts, right):
    total = jnp.dot(parts[2], right, preferred_element_type=F32)
    total = total + jnp.dot(parts[1], right, preferred_element_type=F32)
    return total + jnp.dot(parts[0], right, preferred_element_type=F32)


def pack_x(load, put):
    for way in range(2):
        for half in range(2):
            put(way * 18 + half * 9, 9, load(0, way, None, half * HALF + (15 if way == 0 else 0)))


def pack_y(load, put):
    lane = lanes_of(HALF)
    last = None
    for way in range(2):
        slab = None
        for p in range(9):
            v = load(1, way, p, HALF if way == 0 else 0, HALF)
            source = 7 if way == 0 else 0
            slot = p if p < 8 else way
            v = roll(v, 16 * (slot - source))
            if p < 8:
                slab = v if slab is None else jnp.where(lane // 16 == slot, v, slab)
            else:
                last = v if last is None else jnp.where(lane // 16 == slot, v, last)
        put(way * HALF, HALF, slab)
    put(2 * HALF, HALF, last)


def pack_z(load, put):
    lane = lanes_of(ROWS) % 16
    for way in range(2):
        slab = None
        for p in range(9):
            v = roll(load(2, way, p, 0, ROWS), p - (15 if way == 0 else 0))
            slab = v if slab is None else jnp.where(lane == p, v, slab)
        put(way, slab)


def slab_face(ref, at, way, p, start):
    if p < 8:
        return roll(ref[at, pl.ds(way * HALF, HALF), :], start - 16 * p)
    return roll(ref[at, pl.ds(2 * HALF, HALF), :], start - 16 * way)


def kernel(
    levels,
    neighbours,
    rates,
    diffusivity,
    stoichiometry,
    pop,
    sca,
    old,
    new,
    out_pop,
    out_sca,
    ret_x,
    ret_y,
    ret_z,
    state,
    first,
    up0,
    up1,
    spec,
    spec2,
    res,
    slopes,
    bx_0,
    bx_1,
    by_0,
    by_1,
    bz_out_0,
    bz_out_1,
    bz_0,
    bz_1,
    sxy_0,
    sxy_1,
    sz_out_0,
    sz_out_1,
    sz_0,
    sz_1,
    rxy,
    rz_out,
    rz,
    send_sem,
    recv_sem,
):
    slots = neighbours.shape[0]
    devices = lax.axis_size("blk")
    me = lax.axis_index("blk")
    layers = devices // 2
    layer = me // 2
    core = me % 2
    partner = 2 * layer + 1 - core
    above = lax.rem(layer + 1, layers)
    below = lax.rem(layer + layers - 1, layers)
    mine = core * slots
    around = 2 * slots
    mesh_targets = ((2 * above, 2 * above + 1), (2 * below, 2 * below + 1))

    barrier = pltpu.get_barrier_semaphore()
    for device in (partner,) + mesh_targets[0] + mesh_targets[1]:
        pl.semaphore_signal(barrier, inc=1, device_id=(device,), device_id_type=MESH)

    counter = [0, 0]

    def send_partner(ref):
        s, r = counter[0], counter[1]
        counter[0] += 1
        counter[1] += 1
        part = ref.at[pl.ds(mine, slots)]
        copy = pltpu.make_async_remote_copy(
            src_ref=part,
            dst_ref=part,
            send_sem=send_sem.at[s],
            recv_sem=recv_sem.at[r],
            device_id=(partner,),
            device_id_type=MESH,
        )
        copy.start()
        other = ref.at[pl.ds(slots - mine, slots)]
        arrival = pltpu.make_async_remote_copy(
            src_ref=other,
            dst_ref=other,
            send_sem=send_sem.at[s],
            recv_sem=recv_sem.at[r],
            device_id=(partner,),
            device_id_type=MESH,
        )

        def wait():
            arrival.wait_recv()
            copy.wait_send()

        return wait

    def send_layers(source, target):
        waits = []
        for way in range(2):
            r = counter[1]
            counter[1] += 2
            for core_to in range(2):
                s = counter[0]
                counter[0] += 1
                copy = pltpu.make_async_remote_copy(
                    src_ref=source.at[way],
                    dst_ref=target.at[way, pl.ds(mine, slots)],
                    send_sem=send_sem.at[s],
                    recv_sem=recv_sem.at[r + core],
                    device_id=(mesh_targets[way][core_to],),
                    device_id_type=MESH,
                )
                copy.start()
                waits.append(copy.wait_send)
                arrival = pltpu.make_async_remote_copy(
                    src_ref=source.at[way],
                    dst_ref=target.at[way, pl.ds(core_to * slots, slots)],
                    send_sem=send_sem.at[s],
                    recv_sem=recv_sem.at[r + core_to],
                    device_id=(mesh_targets[way][core_to],),
                    device_id_type=MESH,
                )
                waits.append(arrival.wait_recv)

        def wait():
            for w in waits:
                w()

        return wait

    def each_block(body):
        def wrapped(b, carry):
            body(b)
            return carry

        lax.fori_loop(0, slots, wrapped, 0)

    def fine_of(b):
        return levels[me * slots + b]

    def place(b, q):
        return lax.rem(neighbours[b, q], around)

    def native(i, half, b):
        return pl.ds(i * 2 * HALF * slots + half * slots + b, HALF, stride=2 * slots)

    def unpack_in(b):
        for half in range(2):
            for i in range(27):
                state[b, pl.ds(ROWS * i + half * HALF, HALF), :] = pop[native(i, half, b), :]
            for m in range(9):
                spec[b, pl.ds(ROWS * m + half * HALF, HALF), :] = sca[native(m, half, b), :]

    each_block(unpack_in)

    def spread_coarse(target, average):
        a = 0.5 * (old[...] + new[...]) if average else old[...]
        row = lax.broadcasted_iota(jnp.int32, (LANES, LANES), 0)
        col = lax.broadcasted_iota(jnp.int32, (LANES, LANES), 1)
        want = (col // 32) * 8 + (col % 16) // 2
        parts = split(a)
        for variant in range(4):
            parity, half = variant // 2, variant % 2
            pick = jnp.where(row == want + parity * 64 + half * 32, 1.0, 0.0).astype(jnp.bfloat16)
            res[pl.ds(0, a.shape[0]), :] = product(parts, pick)

            def scatter(b, carry):
                for chunk in range(4):
                    v = res[pl.ds(chunk * slots + b, 27, stride=4 * slots), :]
                    x = 2 * (2 * chunk + parity)
                    target[b, pl.ds(half * HALF + x, 27, stride=ROWS), :] = v
                    target[b, pl.ds(half * HALF + x + 1, 27, stride=ROWS), :] = v
                return carry

            lax.fori_loop(0, slots, scatter, 0)

    spread_coarse(up0, False)

    def population_load(b, spread):
        fine = fine_of(b)

        def load(dim, way, p, start, size=None):
            movers = MOVERS[dim][way]
            if p is None:
                at = pl.ds(ROWS * movers[0] + start, 9, stride=ROWS)
                return jnp.where(flag(fine, 9), state[b, at, :], spread[b, at, :])
            at = pl.ds(ROWS * movers[p] + start, size)
            return jnp.where(flag(fine, size), state[b, at, :], spread[b, at, :])

        return load

    def return_load(b):
        fine = fine_of(b)

        def load(dim, way, p, start, size=None):
            movers = MOVERS[dim][way]
            if p is None:
                at = pl.ds(ROWS * movers[0] + start, 9, stride=ROWS)
                rows = 9
            else:
                at = pl.ds(ROWS * movers[p] + start, size)
                rows = size
            return jnp.where(flag(fine, rows), 0.5 * first[b, at, :] + 0.5 * state[b, at, :], 0.0)

        return load

    def scalar_load(b, source):
        def load(dim, way, p, start, size=None):
            if p is None:
                return source[b, pl.ds(start, 9, stride=ROWS), :]
            return source[b, pl.ds(ROWS * p + start, size), :]

        return load

    def putter(ref, at, base=0):
        def put(start, size, value):
            ref[at, pl.ds(base + start, size), :] = value

        return put

    def putter_z(ref, b):
        def put(way, value):
            ref[way, b] = value

        return put

    def collide(keep):
        scale = [rates[k] * (3.375 / 216.0 * 2.0 ** sum(1 for d in (9, 3, 1) if (k // d) % 3)) for k in range(27)]

        def one(t, carry):
            b = t // 4
            base = pl.multiple_of((t % 4) * 8, 8)

            def at(i):
                return pl.ds(base + ROWS * i, 8)

            g = [state[b, at(i), :] for i in range(27)]
            m = along(along(along(g, 2, to_moments), 1, to_moments), 0, to_moments)
            rho = m[0]
            jx, jy, jz = m[9], m[3], m[1]
            unit = 1.0 / 216.0
            hx, hy, hz = jx * unit, jy * unit, jz * unit
            third = 1.0 / 3.0
            qx, qy, qz = jx * hx, jy * hy, jz * hz
            eq = [None] * 27
            eq[0] = rho
            eq[9], eq[3], eq[1] = jx, jy, jz
            rho3 = rho * third
            eq[18], eq[6], eq[2] = rho3 + qx, rho3 + qy, rho3 + qz
            xy, xz, yz = jx * hy, jx * hz, jy * hz
            eq[12], eq[10], eq[4] = xy, xz, yz
            jx3, jy3, jz3 = jx * third, jy * third, jz * third
            eq[21], eq[19] = jy3, jz3
            eq[15], eq[7] = jx3, jz3
            eq[11], eq[5] = jx3, jy3
            rho9 = rho3 * third
            qx3, qy3, qz3 = qx * third, qy * third, qz * third
            eq[24] = rho9 + qx3 + qy3
            eq[20] = rho9 + qx3 + qz3
            eq[8] = rho9 + qy3 + qz3
            eq[22], eq[16], eq[14] = yz * third, xz * third, xy * third
            eq[25], eq[23], eq[17] = jz3 * third, jy3 * third, jx3 * third
            eq[26] = (rho9 + qx3 + qy3 + qz3) * third
            delta = [
                scale[k] * (m[k] if eq[k] is None else m[k] - eq[k]) for k in range(27)
            ]
            back = along(along(along(delta, 0, from_moments), 1, from_moments), 2, from_moments)
            for i in range(27):
                post = state[b, at(i), :] - back[i]
                state[b, at(i), :] = post
                if keep:
                    first[b, at(i), :] = post
            return carry

        lax.fori_loop(0, slots * 4, one, 0)

    def shift_x(b):
        for p in range(9):
            for half in range(2):
                up = ROWS * MOVERS[0][0][p] + half * HALF
                down = ROWS * MOVERS[0][1][p] + half * HALF
                v = state[b, pl.ds(up, 15), :]
                w = state[b, pl.ds(down + 1, 15), :]
                state[b, pl.ds(up + 1, 15), :] = v
                state[b, pl.ds(down, 15), :] = w

    def enter_x(b, recv):
        low, high = place(b, 0), place(b, 1)
        for half in range(2):
            state[b, pl.ds(ROWS * 18 + half * HALF, 9, stride=ROWS), :] = recv[
                low, pl.ds(half * 9, 9), :
            ]
            state[b, pl.ds(half * HALF + 15, 9, stride=ROWS), :] = recv[
                high, pl.ds(18 + half * 9, 9), :
            ]

    def shift_y(b):
        lane = lanes_of(HALF)
        for p in range(9):
            even = pl.ds(ROWS * MOVERS[1][0][p], HALF)
            odd = pl.ds(ROWS * MOVERS[1][0][p] + HALF, HALF)
            e, o = roll(state[b, even, :], 16), roll(state[b, odd, :], 16)
            state[b, odd, :] = jnp.where(lane < 16, e, o)
            state[b, even, :] = e
            even = pl.ds(ROWS * MOVERS[1][1][p], HALF)
            odd = pl.ds(ROWS * MOVERS[1][1][p] + HALF, HALF)
            e, o = roll(state[b, even, :], -16), roll(state[b, odd, :], -16)
            state[b, even, :] = jnp.where(lane >= 112, o, e)
            state[b, odd, :] = o

    def enter_y(b, recv):
        lane = lanes_of(HALF)
        low, high = place(b, 2), place(b, 3)
        for p in range(9):
            at = pl.ds(ROWS * MOVERS[1][0][p], HALF)
            state[b, at, :] = jnp.where(lane < 16, slab_face(recv, low, 0, p, 0), state[b, at, :])
            at = pl.ds(ROWS * MOVERS[1][1][p] + HALF, HALF)
            state[b, at, :] = jnp.where(
                lane >= 112, slab_face(recv, high, 1, p, 112), state[b, at, :]
            )

    def shift_z(b):
        for p in range(9):
            at = pl.ds(ROWS * MOVERS[2][0][p], ROWS)
            state[b, at, :] = roll(state[b, at, :], 1)
            at = pl.ds(ROWS * MOVERS[2][1][p], ROWS)
            state[b, at, :] = roll(state[b, at, :], -1)

    def enter_z(b, recv):
        lane = lanes_of(ROWS) % 16
        low = recv[0, place(b, 4)]
        high = recv[1, place(b, 5)]
        for p in range(9):
            at = pl.ds(ROWS * MOVERS[2][0][p], ROWS)
            state[b, at, :] = jnp.where(lane == 0, roll(low, -p), state[b, at, :])
            at = pl.ds(ROWS * MOVERS[2][1][p], ROWS)
            state[b, at, :] = jnp.where(lane == 15, roll(high, 15 - p), state[b, at, :])

    def prepare(source, target, recv, recv_z):
        def body(b):
            row = lax.broadcasted_iota(jnp.int32, (HALF, LANES), 0)
            lane = lanes_of(HALF)
            near = lane % 16
            known = [flag(levels[neighbours[b, q]], HALF) for q in range(6)]
            spot = [place(b, q) for q in range(6)]
            e8 = [source[b, pl.ds(ROWS * 8 + h * HALF, HALF), :] for h in range(2)]
            burn = [
                source[b, pl.ds(h * HALF, HALF), :]
                * source[b, pl.ds(ROWS + h * HALF, HALF), :]
                * jnp.exp(4.0 * (e8[h] - 1.0))
                for h in range(2)
            ]
            for m in range(9):
                e = source[b, pl.ds(ROWS * m, HALF), :]
                o = source[b, pl.ds(ROWS * m + HALF, HALF), :]
                pair = (e, o)
                up_y, down_y = roll(e, -16), roll(o, -16)
                up_y = (
                    jnp.where(lane >= 112, down_y, up_y),
                    jnp.where(
                        lane >= 112,
                        jnp.where(known[3], slab_face(recv.at[:, pl.ds(XR, YR)], spot[3], 1, m, 112), o),
                        down_y,
                    ),
                )
                re, ro = roll(e, 16), roll(o, 16)
                down_y = (
                    jnp.where(
                        lane < 16,
                        jnp.where(known[2], slab_face(recv.at[:, pl.ds(XR, YR)], spot[2], 0, m, 0), e),
                        re,
                    ),
                    jnp.where(lane < 16, re, ro),
                )
                for half in range(2):
                    v = pair[half]
                    line = recv[spot[0], pl.ds(half * 9 + m, 1), :]
                    face = jnp.where(known[0], jnp.broadcast_to(line, v.shape), v)
                    down_x = jnp.where(row == 0, face, roll(v, 1, 0))
                    line = recv[spot[1], pl.ds(18 + half * 9 + m, 1), :]
                    face = jnp.where(known[1], jnp.broadcast_to(line, v.shape), v)
                    up_x = jnp.where(row == 15, face, roll(v, -1, 0))
                    face = roll(recv_z[0, spot[4], pl.ds(half * HALF, HALF), :], -m)
                    down_z = jnp.where(near == 0, jnp.where(known[4], face, v), roll(v, 1))
                    face = roll(recv_z[1, spot[5], pl.ds(half * HALF, HALF), :], 15 - m)
                    up_z = jnp.where(near == 15, jnp.where(known[5], face, v), roll(v, -1))
                    at = pl.ds(ROWS * m + half * HALF, HALF)
                    slopes[0, b, at, :] = 0.5 * (up_x - down_x)
                    slopes[1, b, at, :] = 0.5 * (up_y[half] - down_y[half])
                    slopes[2, b, at, :] = 0.5 * (up_z - down_z)
                    spread = (up_x + down_x) + (up_y[half] + down_y[half]) + (up_z + down_z) - 6.0 * v
                    target[b, at, :] = v + diffusivity[m] * spread + stoichiometry[m] * burn[half]

        each_block(body)

    def finish(target):
        def body(b):
            drift = []
            for half in range(2):

                def get(i):
                    return state[b, pl.ds(ROWS * i + half * HALF, HALF), :]

                g = [get(i) for i in range(27)]
                weighted = lambda a, c, f: (a + f) * (1.0 / 6.0) + c * (2.0 / 3.0)
                slope = lambda a, f: (f - a) * (1.0 / 6.0)
                zsum = [weighted(g[3 * k], g[3 * k + 1], g[3 * k + 2]) for k in range(9)]
                zdif = [slope(g[3 * k], g[3 * k + 2]) for k in range(9)]
                ysum = [weighted(zsum[3 * k], zsum[3 * k + 1], zsum[3 * k + 2]) for k in range(3)]
                ydif = [slope(zsum[3 * k], zsum[3 * k + 2]) for k in range(3)]
                zrow = [weighted(zdif[3 * k], zdif[3 * k + 1], zdif[3 * k + 2]) for k in range(3)]
                drift.append((slope(ysum[0], ysum[2]), weighted(*ydif), weighted(*zrow)))
            for m in range(9):
                for half in range(2):
                    at = pl.ds(ROWS * m + half * HALF, HALF)
                    jx, jy, jz = drift[half]
                    target[b, at, :] = target[b, at, :] - (
                        jx * slopes[0, b, at, :] + jy * slopes[1, b, at, :] + jz * slopes[2, b, at, :]
                    )

        each_block(body)

    pl.semaphore_wait(barrier, 5)
    last_wait = None
    for substep in range(2):
        spread = (up0, up1)[substep]
        source, target = (spec, spec2) if substep == 0 else (spec2, spec)
        cx, cy, cz_out, cz = ((bx_0, by_0, bz_out_0, bz_0), (bx_1, by_1, bz_out_1, bz_1))[substep]
        cs, cs_out, cs_z = ((sxy_0, sz_out_0, sz_0), (sxy_1, sz_out_1, sz_1))[substep]

        def pack_scalars(b):
            load = scalar_load(b, source)
            pack_x(load, putter(cs, mine + b))
            pack_y(load, putter(cs, mine + b, XR))
            pack_z(load, putter_z(cs_out, b))

        collide(substep == 0)
        each_block(lambda b: pack_x(population_load(b, spread), putter(cx, mine + b)))
        wait = send_partner(cx)
        if substep == 1:

            def pack_return(b):
                load = return_load(b)
                pack_x(load, putter(rxy, mine + b))
                pack_y(load, putter(rxy, mine + b, XR))
                pack_z(load, putter_z(rz_out, b))

            each_block(pack_return)
            wait_r = send_partner(rxy)
            wait_rz = send_layers(rz_out, rz)
        else:
            each_block(pack_scalars)
            wait_s = send_partner(cs)
            wait_sz = send_layers(cs_out, cs_z)
        each_block(shift_x)
        wait()
        each_block(lambda b: enter_x(b, cx))
        each_block(lambda b: pack_y(population_load(b, spread), putter(cy, mine + b)))
        wait = send_partner(cy)
        if substep == 1:
            each_block(pack_scalars)
            wait_s = send_partner(cs)
            wait_sz = send_layers(cs_out, cs_z)
        else:
            spread_coarse(up1, True)
        each_block(shift_y)
        wait()
        each_block(lambda b: enter_y(b, cy))
        each_block(lambda b: pack_z(population_load(b, spread), putter_z(cz_out, b)))
        wait = send_layers(cz_out, cz)
        each_block(shift_z)
        wait_s()
        wait_sz()
        prepare(source, target, cs, cs_z)
        wait()
        each_block(lambda b: enter_z(b, cz))
        finish(target)
    wait_r()
    wait_rz()

    def pack_out(b):
        fine = flag(fine_of(b), HALF)
        for half in range(2):
            for i in range(27):
                at = native(i, half, b)
                out_pop[at, :] = jnp.where(
                    fine, state[b, pl.ds(ROWS * i + half * HALF, HALF), :], pop[at, :]
                )
            for m in range(9):
                at = native(m, half, b)
                out_sca[at, :] = jnp.where(
                    fine, spec[b, pl.ds(ROWS * m + half * HALF, HALF), :], sca[at, :]
                )
        for way in range(2):
            at = place(b, way)
            ret_x[0, b, way, pl.ds(0, 9), :] = rxy[at, pl.ds(18 * way, 9), :]
            ret_x[1, b, way, pl.ds(0, 9), :] = rxy[at, pl.ds(18 * way + 9, 9), :]
            at = place(b, 2 + way)
            ret_y[b, way, pl.ds(0, HALF), :] = rxy[at, pl.ds(XR + HALF * way, HALF), :]
            ret_y[b, way, pl.ds(HALF, HALF), :] = rxy[at, pl.ds(XR + 2 * HALF, HALF), :]
            ret_z[b, way] = rz[way, place(b, 4 + way)]

    each_block(pack_out)


def means_kernel(levels, ret_x, ret_y, ret_z, out, turned):
    slots = out.shape[0]
    first = lax.axis_index("blk") * slots
    groups = slots // 2

    def mask(b, rows):
        return jnp.broadcast_to(levels[first + b], (rows, 64)) == 1

    def grid(rows, columns):
        return tuple(lax.broadcasted_iota(jnp.int32, (rows, columns), d) for d in range(2))

    def pick(cond):
        return jnp.where(cond, 0.25, 0.0).astype(jnp.bfloat16)

    k, n = grid(LANES, 64)
    total = None
    for half in range(2):
        right = pick(n == half * 32 + (k // 32) * 8 + (k % 16) // 2)
        v = ret_x[half].reshape(slots * 2 * 16, LANES)
        part = product(split(v), right)
        total = part if total is None else total + part
    for b in range(slots):
        for way in range(2):
            v = total[(b * 2 + way) * 16 : (b * 2 + way) * 16 + 9]
            out[b, way] = jnp.where(mask(b, 9), 0.0, v)

    k, n = grid(LANES, 512)
    for g in range(groups):
        turned[pl.ds(g * LANES, LANES), :] = (
            ret_y[pl.ds(2 * g, 2)].reshape(LANES, LANES).T
        )
    total = None
    for z in range(8):
        left = (
            turned[pl.ds(2 * z, 8 * groups, stride=16), :]
            + turned[pl.ds(2 * z + 1, 8 * groups, stride=16), :]
        )
        right = pick(
            (k // 32 == (n % 256) // 64)
            & ((k % 32) // 16 == n // 256)
            & (n % 64 == ((k % 16) // 2) * 8 + z)
        )
        part = product(split(left), right)
        total = part if total is None else total + part
    for b in range(slots):
        for way in range(2):
            g, at = b // 2, (b % 2) * 2 + way
            v = total[g * 8 : g * 8 + 8, at * 64 : at * 64 + 64]
            w = total[g * 8 + way : g * 8 + way + 1, 256 + at * 64 : 256 + at * 64 + 64]
            out[b, 2 + way, pl.ds(0, 8), :] = jnp.where(mask(b, 8), 0.0, v)
            out[b, 2 + way, pl.ds(8, 1), :] = jnp.where(mask(b, 1), 0.0, w)

    k, n = grid(LANES, 256)
    total = [None] * groups
    for g in range(groups):
        turned[pl.ds(g * LANES, LANES), :] = (
            ret_z[pl.ds(2 * g, 2)].reshape(LANES, LANES).T
        )
    for y in range(4):
        right = pick(
            (k // 32 == n // 64)
            & (n % 64 == ((k % 16) // 2) * 8 + ((k % 32) // 16) * 4 + y)
        )
        for g in range(groups):
            base = g * LANES + 32 * y
            left = turned[pl.ds(base, 16), :] + turned[pl.ds(base + 16, 16), :]
            part = product(split(left), right)
            total[g] = part if total[g] is None else total[g] + part
    for b in range(slots):
        for way in range(2):
            at = (b % 2) * 2 + way
            v = total[b // 2][0:9, at * 64 : at * 64 + 64]
            out[b, 4 + way] = jnp.where(mask(b, 9), 0.0, v)


def rows_of(array):
    slots, k, cells = array.shape
    v = array.reshape(slots, k, cells // LANES, LANES).transpose(1, 2, 0, 3)
    return v.reshape(-1, LANES)


def array_of(rows, slots, k):
    v = rows.reshape(k, -1, slots, LANES).transpose(2, 0, 1, 3)
    return v.reshape(slots, k, -1)


def local(
    populations,
    scalars,
    coarse_old,
    coarse_new,
    levels,
    neighbours,
    relax_rates,
    diffusivity,
    stoichiometry,
):
    slots = populations.shape[0]
    vmem = pl.BlockSpec(memory_space=pltpu.VMEM)
    smem = pl.BlockSpec(memory_space=pltpu.SMEM)
    shape = jax.ShapeDtypeStruct
    layer = 2 * slots
    outs = pl.pallas_call(
        kernel,
        out_shape=(
            shape((slots * 27 * ROWS, LANES), F32),
            shape((slots * 9 * ROWS, LANES), F32),
            shape((2, slots, 2, 16, LANES), F32),
            shape((slots, 2, 32, LANES), F32),
            shape((slots, 2, 32, LANES), F32),
        ),
        in_specs=[smem] * 5 + [vmem] * 4,
        out_specs=[vmem] * 5,
        scratch_shapes=[
            pltpu.VMEM((slots, POP_ROWS, LANES), F32),
            pltpu.VMEM((slots, POP_ROWS, LANES), F32),
            pltpu.VMEM((slots, POP_ROWS, LANES), F32),
            pltpu.VMEM((slots, POP_ROWS, LANES), F32),
            pltpu.VMEM((slots, SCA_ROWS, LANES), F32),
            pltpu.VMEM((slots, SCA_ROWS, LANES), F32),
            pltpu.VMEM((slots * 4 * ROWS, LANES), F32),
            pltpu.VMEM((3, slots, 9 * ROWS, LANES), F32),
            pltpu.VMEM((layer + 1, XR, LANES), F32),
            pltpu.VMEM((layer + 1, XR, LANES), F32),
            pltpu.VMEM((layer, YR, LANES), F32),
            pltpu.VMEM((layer, YR, LANES), F32),
            pltpu.VMEM((2, slots, ROWS, LANES), F32),
            pltpu.VMEM((2, slots, ROWS, LANES), F32),
            pltpu.VMEM((2, layer, ROWS, LANES), F32),
            pltpu.VMEM((2, layer, ROWS, LANES), F32),
            pltpu.VMEM((layer, XR + YR, LANES), F32),
            pltpu.VMEM((layer, XR + YR, LANES), F32),
            pltpu.VMEM((2, slots, ROWS, LANES), F32),
            pltpu.VMEM((2, slots, ROWS, LANES), F32),
            pltpu.VMEM((2, layer, ROWS, LANES), F32),
            pltpu.VMEM((2, layer, ROWS, LANES), F32),
            pltpu.VMEM((layer, XR + YR, LANES), F32),
            pltpu.VMEM((2, slots, ROWS, LANES), F32),
            pltpu.VMEM((2, layer, ROWS, LANES), F32),
            pltpu.SemaphoreType.DMA((32,)),
            pltpu.SemaphoreType.DMA((32,)),
        ],
        compiler_params=pltpu.CompilerParams(
            collective_id=0, has_side_effects=True, vmem_limit_bytes=56 << 20
        ),
    )(
        levels,
        neighbours,
        relax_rates,
        diffusivity,
        stoichiometry,
        rows_of(populations),
        rows_of(scalars),
        rows_of(coarse_old),
        rows_of(coarse_new),
    )
    new_populations, new_scalars, ret_x, ret_y, ret_z = outs
    back = pl.pallas_call(
        means_kernel,
        out_shape=shape((slots, 6, 9, 64), F32),
        in_specs=[smem] + [vmem] * 3,
        out_specs=vmem,
        scratch_shapes=[pltpu.VMEM((slots // 2 * LANES, LANES), F32)],
    )(levels, ret_x, ret_y, ret_z)
    return (
        array_of(new_populations, slots, 27),
        array_of(new_scalars, slots, 9),
        back.reshape(slots, -1),
    )


def solution(mesh):
    in_specs = (
        P("blk", None, None),
        P("blk", None, None),
        P("blk", None, None),
        P("blk", None, None),
        P(),
        P("blk", None),
        P(),
        P(),
        P(),
    )
    out_specs = (P("blk", None, None), P("blk", None, None), P("blk", None))
    return jax.shard_map(local, mesh=mesh, in_specs=in_specs, out_specs=out_specs, check_vma=False)
```

```python
import jax
import jax.numpy as jnp
import numpy as np
from jax import lax
from jax.experimental import pallas as pl
from jax.experimental.pallas import tpu as pltpu
from jax.sharding import PartitionSpec as P

F32 = jnp.float32
MESH = pl.DeviceIdType.MESH
LANES = 128
ROWS = 32
HALF = 16
MOVERS = (
    (tuple(18 + p for p in range(9)), tuple(p for p in range(9))),
    (
        tuple(9 * (p // 3) + 6 + p % 3 for p in range(9)),
        tuple(9 * (p // 3) + p % 3 for p in range(9)),
    ),
    (tuple(3 * p + 2 for p in range(9)), tuple(3 * p for p in range(9))),
)
SCALAR_ROWS = (tuple(range(9)), tuple(range(9)))
XR = 40
POP_ROWS = 36 * 32
SCA_ROWS = 20 * 32
YR = 48


def lanes_of(rows):
    return lax.broadcasted_iota(jnp.int32, (rows, LANES), 1)


def flag(value, rows):
    return jnp.broadcast_to(value, (rows, LANES)) == 1


def roll(v, by, axis=1):
    size = v.shape[axis]
    by = by % size
    return v if by == 0 else pltpu.roll(v, by, axis)


def along(values, dim, func):
    out = [None] * 27
    step = (9, 3, 1)[dim]
    for base in range(27):
        if (base // step) % 3 == 0:
            a, b, c = func(values[base], values[base + step], values[base + 2 * step])
            out[base], out[base + step], out[base + 2 * step] = a, b, c
    return out


def to_moments(low, mid, high):
    both = low + high
    return both + 4.0 * mid, high - low, both


def from_moments(m0, m1, m2):
    return m2 - m1, m0 - 0.5 * m2, m1 + m2


def split(a):
    a0 = a.astype(jnp.bfloat16)
    rest = a - a0.astype(F32)
    a1 = rest.astype(jnp.bfloat16)
    return a0, a1, (rest - a1.astype(F32)).astype(jnp.bfloat16)


def product(parts, right):
    total = jnp.dot(parts[2], right, preferred_element_type=F32)
    total = total + jnp.dot(parts[1], right, preferred_element_type=F32)
    return total + jnp.dot(parts[0], right, preferred_element_type=F32)


def pack_x(load, put):
    for way in range(2):
        for half in range(2):
            put(way * 18 + half * 9, 9, load(0, way, None, half * HALF + (15 if way == 0 else 0)))


def pack_y(load, put):
    lane = lanes_of(HALF)
    last = None
    for way in range(2):
        slab = None
        for p in range(9):
            v = load(1, way, p, HALF if way == 0 else 0, HALF)
            source = 7 if way == 0 else 0
            slot = p if p < 8 else way
            v = roll(v, 16 * (slot - source))
            if p < 8:
                slab = v if slab is None else jnp.where(lane // 16 == slot, v, slab)
            else:
                last = v if last is None else jnp.where(lane // 16 == slot, v, last)
        put(way * HALF, HALF, slab)
    put(2 * HALF, HALF, last)


def pack_z(load, put):
    lane = lanes_of(ROWS) % 16
    for way in range(2):
        slab = None
        for p in range(9):
            v = roll(load(2, way, p, 0, ROWS), p - (15 if way == 0 else 0))
            slab = v if slab is None else jnp.where(lane == p, v, slab)
        put(way, slab)


def slab_face(ref, at, way, p, start):
    if p < 8:
        return roll(ref[at, pl.ds(way * HALF, HALF), :], start - 16 * p)
    return roll(ref[at, pl.ds(2 * HALF, HALF), :], start - 16 * way)


def kernel(
    levels,
    neighbours,
    rates,
    diffusivity,
    stoichiometry,
    pop,
    sca,
    old,
    new,
    out_pop,
    out_sca,
    ret_x,
    ret_y,
    ret_z,
    state,
    first,
    up0,
    up1,
    spec,
    spec2,
    res,
    slopes,
    bx_0,
    bx_1,
    by_0,
    by_1,
    bz_out_0,
    bz_out_1,
    bz_0,
    bz_1,
    sxy_0,
    sxy_1,
    sz_out_0,
    sz_out_1,
    sz_0,
    sz_1,
    rxy,
    rz_out,
    rz,
    send_sem,
    recv_sem,
):
    slots = neighbours.shape[0]
    devices = lax.axis_size("blk")
    me = lax.axis_index("blk")
    layers = devices // 2
    layer = me // 2
    core = me % 2
    partner = 2 * layer + 1 - core
    above = lax.rem(layer + 1, layers)
    below = lax.rem(layer + layers - 1, layers)
    mine = core * slots
    around = 2 * slots
    mesh_targets = (2 * above + core, 2 * below + core)

    barrier = pltpu.get_barrier_semaphore()
    for device in (partner,) + mesh_targets:
        pl.semaphore_signal(barrier, inc=1, device_id=(device,), device_id_type=MESH)

    counter = [0, 0]

    def send_partner(ref):
        s, r = counter[0], counter[1]
        counter[0] += 1
        counter[1] += 1
        part = ref.at[pl.ds(mine, slots)]
        copy = pltpu.make_async_remote_copy(
            src_ref=part,
            dst_ref=part,
            send_sem=send_sem.at[s],
            recv_sem=recv_sem.at[r],
            device_id=(partner,),
            device_id_type=MESH,
        )
        copy.start()
        other = ref.at[pl.ds(slots - mine, slots)]
        arrival = pltpu.make_async_remote_copy(
            src_ref=other,
            dst_ref=other,
            send_sem=send_sem.at[s],
            recv_sem=recv_sem.at[r],
            device_id=(partner,),
            device_id_type=MESH,
        )

        def wait():
            arrival.wait_recv()
            copy.wait_send()

        return wait

    def send_layers(source, target):
        copies = []
        for way in range(2):
            s, r = counter[0], counter[1]
            counter[0] += 1
            counter[1] += 1
            copy = pltpu.make_async_remote_copy(
                src_ref=source.at[way],
                dst_ref=target.at[way, pl.ds(mine, slots)],
                send_sem=send_sem.at[s],
                recv_sem=recv_sem.at[r],
                device_id=(mesh_targets[way],),
                device_id_type=MESH,
            )
            copy.start()
            copies.append(copy)

        def relay():
            waits = []
            for way in range(2):
                copies[way].wait_recv()
                waits.append(send_partner(target.at[way]))

            def wait():
                for way in range(2):
                    copies[way].wait_send()
                    waits[way]()

            return wait

        return relay

    def each_block(body):
        def wrapped(b, carry):
            body(b)
            return carry

        lax.fori_loop(0, slots, wrapped, 0)

    def fine_of(b):
        return levels[me * slots + b]

    def place(b, q):
        return lax.rem(neighbours[b, q], around)

    def native(i, half, b):
        return pl.ds(i * 2 * HALF * slots + half * slots + b, HALF, stride=2 * slots)

    def unpack_in(b):
        for half in range(2):
            for i in range(27):
                state[b, pl.ds(ROWS * i + half * HALF, HALF), :] = pop[native(i, half, b), :]
            for m in range(9):
                spec[b, pl.ds(ROWS * m + half * HALF, HALF), :] = sca[native(m, half, b), :]

    each_block(unpack_in)

    def spread_values(average):
        a = 0.5 * (old[...] + new[...]) if average else old[...]
        row = lax.broadcasted_iota(jnp.int32, (LANES, LANES), 0)
        col = lax.broadcasted_iota(jnp.int32, (LANES, LANES), 1)
        want = (col // 32) * 8 + (col % 16) // 2
        parts = split(a)
        for variant in range(4):
            at = variant // 2 * 64 + variant % 2 * 32
            pick = jnp.where(row == want + at, 1.0, 0.0).astype(jnp.bfloat16)
            res[variant, pl.ds(0, a.shape[0]), :] = product(parts, pick)

    def spread_rows(target, b, variant, chunk, xs):
        v = res[variant, pl.ds(chunk * slots + b, 27, stride=4 * slots), :]
        for x in xs:
            target[b, pl.ds(variant % 2 * HALF + x, 27, stride=ROWS), :] = v

    def spread_ends(target):
        def body(b):
            for half in range(2):
                spread_rows(target, b, half, 0, (0,))
                spread_rows(target, b, 2 + half, 3, (15,))

        each_block(body)

    def spread_all(target):
        def body(b):
            for variant in range(4):
                for chunk in range(4):
                    x = 2 * (2 * chunk + variant // 2)
                    spread_rows(target, b, variant, chunk, (x, x + 1))

        each_block(body)

    spread_values(False)
    spread_ends(up0)

    def population_load(b, spread):
        fine = fine_of(b)

        def load(dim, way, p, start, size=None):
            movers = MOVERS[dim][way]
            if p is None:
                at = pl.ds(ROWS * movers[0] + start, 9, stride=ROWS)
                return jnp.where(flag(fine, 9), state[b, at, :], spread[b, at, :])
            at = pl.ds(ROWS * movers[p] + start, size)
            return jnp.where(flag(fine, size), state[b, at, :], spread[b, at, :])

        return load

    def return_load(b):
        fine = fine_of(b)

        def load(dim, way, p, start, size=None):
            movers = MOVERS[dim][way]
            if p is None:
                at = pl.ds(ROWS * movers[0] + start, 9, stride=ROWS)
                rows = 9
            else:
                at = pl.ds(ROWS * movers[p] + start, size)
                rows = size
            return jnp.where(flag(fine, rows), 0.5 * first[b, at, :] + 0.5 * state[b, at, :], 0.0)

        return load

    def scalar_load(b, source):
        def load(dim, way, p, start, size=None):
            if p is None:
                return source[b, pl.ds(start, 9, stride=ROWS), :]
            return source[b, pl.ds(ROWS * p + start, size), :]

        return load

    def putter(ref, at, base=0):
        def put(start, size, value):
            ref[at, pl.ds(base + start, size), :] = value

        return put

    def putter_z(ref, b):
        def put(way, value):
            ref[way, b] = value

        return put

    def collide(keep):
        scale = [rates[k] * (3.375 / 216.0 * 2.0 ** sum(1 for d in (9, 3, 1) if (k // d) % 3)) for k in range(27)]

        def one(t, carry):
            b = t // 4
            base = pl.multiple_of((t % 4) * 8, 8)

            def at(i):
                return pl.ds(base + ROWS * i, 8)

            g = [state[b, at(i), :] for i in range(27)]
            m = along(along(along(g, 2, to_moments), 1, to_moments), 0, to_moments)
            rho = m[0]
            jx, jy, jz = m[9], m[3], m[1]
            unit = 1.0 / 216.0
            hx, hy, hz = jx * unit, jy * unit, jz * unit
            third = 1.0 / 3.0
            qx, qy, qz = jx * hx, jy * hy, jz * hz
            eq = [None] * 27
            eq[0] = rho
            eq[9], eq[3], eq[1] = jx, jy, jz
            rho3 = rho * third
            eq[18], eq[6], eq[2] = rho3 + qx, rho3 + qy, rho3 + qz
            xy, xz, yz = jx * hy, jx * hz, jy * hz
            eq[12], eq[10], eq[4] = xy, xz, yz
            jx3, jy3, jz3 = jx * third, jy * third, jz * third
            eq[21], eq[19] = jy3, jz3
            eq[15], eq[7] = jx3, jz3
            eq[11], eq[5] = jx3, jy3
            rho9 = rho3 * third
            qx3, qy3, qz3 = qx * third, qy * third, qz * third
            eq[24] = rho9 + qx3 + qy3
            eq[20] = rho9 + qx3 + qz3
            eq[8] = rho9 + qy3 + qz3
            eq[22], eq[16], eq[14] = yz * third, xz * third, xy * third
            eq[25], eq[23], eq[17] = jz3 * third, jy3 * third, jx3 * third
            eq[26] = (rho9 + qx3 + qy3 + qz3) * third
            delta = [
                scale[k] * (m[k] if eq[k] is None else m[k] - eq[k]) for k in range(27)
            ]
            back = along(along(along(delta, 0, from_moments), 1, from_moments), 2, from_moments)
            for i in range(27):
                post = state[b, at(i), :] - back[i]
                state[b, at(i), :] = post
                if keep:
                    first[b, at(i), :] = post
            return carry

        lax.fori_loop(0, slots * 4, one, 0)

    def shift_x(b):
        for p in range(9):
            for half in range(2):
                up = ROWS * MOVERS[0][0][p] + half * HALF
                down = ROWS * MOVERS[0][1][p] + half * HALF
                v = state[b, pl.ds(up, 15), :]
                w = state[b, pl.ds(down + 1, 15), :]
                state[b, pl.ds(up + 1, 15), :] = v
                state[b, pl.ds(down, 15), :] = w

    def enter_x(b, recv):
        low, high = place(b, 0), place(b, 1)
        for half in range(2):
            state[b, pl.ds(ROWS * 18 + half * HALF, 9, stride=ROWS), :] = recv[
                low, pl.ds(half * 9, 9), :
            ]
            state[b, pl.ds(half * HALF + 15, 9, stride=ROWS), :] = recv[
                high, pl.ds(18 + half * 9, 9), :
            ]

    def shift_y(b):
        lane = lanes_of(HALF)
        for p in range(9):
            even = pl.ds(ROWS * MOVERS[1][0][p], HALF)
            odd = pl.ds(ROWS * MOVERS[1][0][p] + HALF, HALF)
            e, o = roll(state[b, even, :], 16), roll(state[b, odd, :], 16)
            state[b, odd, :] = jnp.where(lane < 16, e, o)
            state[b, even, :] = e
            even = pl.ds(ROWS * MOVERS[1][1][p], HALF)
            odd = pl.ds(ROWS * MOVERS[1][1][p] + HALF, HALF)
            e, o = roll(state[b, even, :], -16), roll(state[b, odd, :], -16)
            state[b, even, :] = jnp.where(lane >= 112, o, e)
            state[b, odd, :] = o

    def enter_y(b, recv):
        lane = lanes_of(HALF)
        low, high = place(b, 2), place(b, 3)
        for p in range(9):
            at = pl.ds(ROWS * MOVERS[1][0][p], HALF)
            state[b, at, :] = jnp.where(lane < 16, slab_face(recv, low, 0, p, 0), state[b, at, :])
            at = pl.ds(ROWS * MOVERS[1][1][p] + HALF, HALF)
            state[b, at, :] = jnp.where(
                lane >= 112, slab_face(recv, high, 1, p, 112), state[b, at, :]
            )

    def shift_z(b):
        for p in range(9):
            at = pl.ds(ROWS * MOVERS[2][0][p], ROWS)
            state[b, at, :] = roll(state[b, at, :], 1)
            at = pl.ds(ROWS * MOVERS[2][1][p], ROWS)
            state[b, at, :] = roll(state[b, at, :], -1)

    def enter_z(b, recv):
        lane = lanes_of(ROWS) % 16
        low = recv[0, place(b, 4)]
        high = recv[1, place(b, 5)]
        for p in range(9):
            at = pl.ds(ROWS * MOVERS[2][0][p], ROWS)
            state[b, at, :] = jnp.where(lane == 0, roll(low, -p), state[b, at, :])
            at = pl.ds(ROWS * MOVERS[2][1][p], ROWS)
            state[b, at, :] = jnp.where(lane == 15, roll(high, 15 - p), state[b, at, :])

    def prepare(source, target, recv, recv_z):
        def body(b):
            row = lax.broadcasted_iota(jnp.int32, (HALF, LANES), 0)
            lane = lanes_of(HALF)
            near = lane % 16
            known = [flag(levels[neighbours[b, q]], HALF) for q in range(6)]
            spot = [place(b, q) for q in range(6)]
            e8 = [source[b, pl.ds(ROWS * 8 + h * HALF, HALF), :] for h in range(2)]
            burn = [
                source[b, pl.ds(h * HALF, HALF), :]
                * source[b, pl.ds(ROWS + h * HALF, HALF), :]
                * jnp.exp(4.0 * (e8[h] - 1.0))
                for h in range(2)
            ]
            for m in range(9):
                e = source[b, pl.ds(ROWS * m, HALF), :]
                o = source[b, pl.ds(ROWS * m + HALF, HALF), :]
                pair = (e, o)
                up_y, down_y = roll(e, -16), roll(o, -16)
                up_y = (
                    jnp.where(lane >= 112, down_y, up_y),
                    jnp.where(
                        lane >= 112,
                        jnp.where(known[3], slab_face(recv.at[:, pl.ds(XR, YR)], spot[3], 1, m, 112), o),
                        down_y,
                    ),
                )
                re, ro = roll(e, 16), roll(o, 16)
                down_y = (
                    jnp.where(
                        lane < 16,
                        jnp.where(known[2], slab_face(recv.at[:, pl.ds(XR, YR)], spot[2], 0, m, 0), e),
                        re,
                    ),
                    jnp.where(lane < 16, re, ro),
                )
                for half in range(2):
                    v = pair[half]
                    line = recv[spot[0], pl.ds(half * 9 + m, 1), :]
                    face = jnp.where(known[0], jnp.broadcast_to(line, v.shape), v)
                    down_x = jnp.where(row == 0, face, roll(v, 1, 0))
                    line = recv[spot[1], pl.ds(18 + half * 9 + m, 1), :]
                    face = jnp.where(known[1], jnp.broadcast_to(line, v.shape), v)
                    up_x = jnp.where(row == 15, face, roll(v, -1, 0))
                    face = roll(recv_z[0, spot[4], pl.ds(half * HALF, HALF), :], -m)
                    down_z = jnp.where(near == 0, jnp.where(known[4], face, v), roll(v, 1))
                    face = roll(recv_z[1, spot[5], pl.ds(half * HALF, HALF), :], 15 - m)
                    up_z = jnp.where(near == 15, jnp.where(known[5], face, v), roll(v, -1))
                    at = pl.ds(ROWS * m + half * HALF, HALF)
                    slopes[0, b, at, :] = 0.5 * (up_x - down_x)
                    slopes[1, b, at, :] = 0.5 * (up_y[half] - down_y[half])
                    slopes[2, b, at, :] = 0.5 * (up_z - down_z)
                    spread = (up_x + down_x) + (up_y[half] + down_y[half]) + (up_z + down_z) - 6.0 * v
                    target[b, at, :] = v + diffusivity[m] * spread + stoichiometry[m] * burn[half]

        each_block(body)

    def finish(target):
        def body(b):
            drift = []
            for half in range(2):

                def get(i):
                    return state[b, pl.ds(ROWS * i + half * HALF, HALF), :]

                g = [get(i) for i in range(27)]
                weighted = lambda a, c, f: (a + f) * (1.0 / 6.0) + c * (2.0 / 3.0)
                slope = lambda a, f: (f - a) * (1.0 / 6.0)
                zsum = [weighted(g[3 * k], g[3 * k + 1], g[3 * k + 2]) for k in range(9)]
                zdif = [slope(g[3 * k], g[3 * k + 2]) for k in range(9)]
                ysum = [weighted(zsum[3 * k], zsum[3 * k + 1], zsum[3 * k + 2]) for k in range(3)]
                ydif = [slope(zsum[3 * k], zsum[3 * k + 2]) for k in range(3)]
                zrow = [weighted(zdif[3 * k], zdif[3 * k + 1], zdif[3 * k + 2]) for k in range(3)]
                drift.append((slope(ysum[0], ysum[2]), weighted(*ydif), weighted(*zrow)))
            for m in range(9):
                for half in range(2):
                    at = pl.ds(ROWS * m + half * HALF, HALF)
                    jx, jy, jz = drift[half]
                    target[b, at, :] = target[b, at, :] - (
                        jx * slopes[0, b, at, :] + jy * slopes[1, b, at, :] + jz * slopes[2, b, at, :]
                    )

        each_block(body)

    pl.semaphore_wait(barrier, 3)
    last_wait = None
    for substep in range(2):
        spread = (up0, up1)[substep]
        source, target = (spec, spec2) if substep == 0 else (spec2, spec)
        cx, cy, cz_out, cz = ((bx_0, by_0, bz_out_0, bz_0), (bx_1, by_1, bz_out_1, bz_1))[substep]
        cs, cs_out, cs_z = ((sxy_0, sz_out_0, sz_0), (sxy_1, sz_out_1, sz_1))[substep]

        def pack_scalars(b):
            load = scalar_load(b, source)
            pack_x(load, putter(cs, mine + b))
            pack_y(load, putter(cs, mine + b, XR))
            pack_z(load, putter_z(cs_out, b))

        collide(substep == 0)
        each_block(lambda b: pack_x(population_load(b, spread), putter(cx, mine + b)))
        wait = send_partner(cx)
        if substep == 1:

            def pack_return(b):
                load = return_load(b)
                pack_x(load, putter(rxy, mine + b))
                pack_y(load, putter(rxy, mine + b, XR))
                pack_z(load, putter_z(rz_out, b))

            each_block(pack_return)
            wait_r = send_partner(rxy)
            relay_rz = send_layers(rz_out, rz)
        else:
            each_block(pack_scalars)
            wait_s = send_partner(cs)
            relay_sz = send_layers(cs_out, cs_z)
            spread_all(up0)
        each_block(shift_x)
        wait()
        each_block(lambda b: enter_x(b, cx))
        each_block(lambda b: pack_y(population_load(b, spread), putter(cy, mine + b)))
        wait = send_partner(cy)
        if substep == 1:
            each_block(pack_scalars)
            wait_s = send_partner(cs)
            relay_sz = send_layers(cs_out, cs_z)
        else:
            spread_values(True)
            spread_all(up1)
        each_block(shift_y)
        wait()
        each_block(lambda b: enter_y(b, cy))
        each_block(lambda b: pack_z(population_load(b, spread), putter_z(cz_out, b)))
        relay = send_layers(cz_out, cz)
        wait_sz = relay_sz()
        each_block(shift_z)
        wait_s()
        wait_sz()
        if substep == 1:
            wait_rz = relay_rz()
        prepare(source, target, cs, cs_z)
        wait = relay()
        wait()
        each_block(lambda b: enter_z(b, cz))
        finish(target)
    wait_r()
    wait_rz()

    def pack_out(b):
        fine = flag(fine_of(b), HALF)
        for half in range(2):
            for i in range(27):
                at = native(i, half, b)
                out_pop[at, :] = jnp.where(
                    fine, state[b, pl.ds(ROWS * i + half * HALF, HALF), :], pop[at, :]
                )
            for m in range(9):
                at = native(m, half, b)
                out_sca[at, :] = jnp.where(
                    fine, spec[b, pl.ds(ROWS * m + half * HALF, HALF), :], sca[at, :]
                )
        for way in range(2):
            at = place(b, way)
            ret_x[0, b, way, pl.ds(0, 9), :] = rxy[at, pl.ds(18 * way, 9), :]
            ret_x[1, b, way, pl.ds(0, 9), :] = rxy[at, pl.ds(18 * way + 9, 9), :]
            at = place(b, 2 + way)
            ret_y[b, way, pl.ds(0, HALF), :] = rxy[at, pl.ds(XR + HALF * way, HALF), :]
            ret_y[b, way, pl.ds(HALF, HALF), :] = rxy[at, pl.ds(XR + 2 * HALF, HALF), :]
            ret_z[b, way] = rz[way, place(b, 4 + way)]

    each_block(pack_out)


def means_kernel(levels, ret_x, ret_y, ret_z, out, turned):
    slots = out.shape[0]
    first = lax.axis_index("blk") * slots
    groups = slots // 2

    def mask(b, rows):
        return jnp.broadcast_to(levels[first + b], (rows, 64)) == 1

    def grid(rows, columns):
        return tuple(lax.broadcasted_iota(jnp.int32, (rows, columns), d) for d in range(2))

    def pick(cond):
        return jnp.where(cond, 0.25, 0.0).astype(jnp.bfloat16)

    k, n = grid(LANES, 64)
    total = None
    for half in range(2):
        right = pick(n == half * 32 + (k // 32) * 8 + (k % 16) // 2)
        v = ret_x[half].reshape(slots * 2 * 16, LANES)
        part = product(split(v), right)
        total = part if total is None else total + part
    for b in range(slots):
        for way in range(2):
            v = total[(b * 2 + way) * 16 : (b * 2 + way) * 16 + 9]
            out[b, way] = jnp.where(mask(b, 9), 0.0, v)

    k, n = grid(LANES, 512)
    for g in range(groups):
        turned[pl.ds(g * LANES, LANES), :] = (
            ret_y[pl.ds(2 * g, 2)].reshape(LANES, LANES).T
        )
    total = None
    for z in range(8):
        left = (
            turned[pl.ds(2 * z, 8 * groups, stride=16), :]
            + turned[pl.ds(2 * z + 1, 8 * groups, stride=16), :]
        )
        right = pick(
            (k // 32 == (n % 256) // 64)
            & ((k % 32) // 16 == n // 256)
            & (n % 64 == ((k % 16) // 2) * 8 + z)
        )
        part = product(split(left), right)
        total = part if total is None else total + part
    for b in range(slots):
        for way in range(2):
            g, at = b // 2, (b % 2) * 2 + way
            v = total[g * 8 : g * 8 + 8, at * 64 : at * 64 + 64]
            w = total[g * 8 + way : g * 8 + way + 1, 256 + at * 64 : 256 + at * 64 + 64]
            out[b, 2 + way, pl.ds(0, 8), :] = jnp.where(mask(b, 8), 0.0, v)
            out[b, 2 + way, pl.ds(8, 1), :] = jnp.where(mask(b, 1), 0.0, w)

    k, n = grid(LANES, 256)
    total = [None] * groups
    for g in range(groups):
        turned[pl.ds(g * LANES, LANES), :] = (
            ret_z[pl.ds(2 * g, 2)].reshape(LANES, LANES).T
        )
    for y in range(4):
        right = pick(
            (k // 32 == n // 64)
            & (n % 64 == ((k % 16) // 2) * 8 + ((k % 32) // 16) * 4 + y)
        )
        for g in range(groups):
            base = g * LANES + 32 * y
            left = turned[pl.ds(base, 16), :] + turned[pl.ds(base + 16, 16), :]
            part = product(split(left), right)
            total[g] = part if total[g] is None else total[g] + part
    for b in range(slots):
        for way in range(2):
            at = (b % 2) * 2 + way
            v = total[b // 2][0:9, at * 64 : at * 64 + 64]
            out[b, 4 + way] = jnp.where(mask(b, 9), 0.0, v)


def rows_of(array):
    slots, k, cells = array.shape
    v = array.reshape(slots, k, cells // LANES, LANES).transpose(1, 2, 0, 3)
    return v.reshape(-1, LANES)


def array_of(rows, slots, k):
    v = rows.reshape(k, -1, slots, LANES).transpose(2, 0, 1, 3)
    return v.reshape(slots, k, -1)


def local(
    populations,
    scalars,
    coarse_old,
    coarse_new,
    levels,
    neighbours,
    relax_rates,
    diffusivity,
    stoichiometry,
):
    slots = populations.shape[0]
    vmem = pl.BlockSpec(memory_space=pltpu.VMEM)
    smem = pl.BlockSpec(memory_space=pltpu.SMEM)
    shape = jax.ShapeDtypeStruct
    layer = 2 * slots
    outs = pl.pallas_call(
        kernel,
        out_shape=(
            shape((slots * 27 * ROWS, LANES), F32),
            shape((slots * 9 * ROWS, LANES), F32),
            shape((2, slots, 2, 16, LANES), F32),
            shape((slots, 2, 32, LANES), F32),
            shape((slots, 2, 32, LANES), F32),
        ),
        in_specs=[smem] * 5 + [vmem] * 4,
        out_specs=[vmem] * 5,
        scratch_shapes=[
            pltpu.VMEM((slots, POP_ROWS, LANES), F32),
            pltpu.VMEM((slots, POP_ROWS, LANES), F32),
            pltpu.VMEM((slots, POP_ROWS, LANES), F32),
            pltpu.VMEM((slots, POP_ROWS, LANES), F32),
            pltpu.VMEM((slots, SCA_ROWS, LANES), F32),
            pltpu.VMEM((slots, SCA_ROWS, LANES), F32),
            pltpu.VMEM((4, slots * 4 * ROWS, LANES), F32),
            pltpu.VMEM((3, slots, 9 * ROWS, LANES), F32),
            pltpu.VMEM((layer + 1, XR, LANES), F32),
            pltpu.VMEM((layer + 1, XR, LANES), F32),
            pltpu.VMEM((layer, YR, LANES), F32),
            pltpu.VMEM((layer, YR, LANES), F32),
            pltpu.VMEM((2, slots, ROWS, LANES), F32),
            pltpu.VMEM((2, slots, ROWS, LANES), F32),
            pltpu.VMEM((2, layer, ROWS, LANES), F32),
            pltpu.VMEM((2, layer, ROWS, LANES), F32),
            pltpu.VMEM((layer, XR + YR, LANES), F32),
            pltpu.VMEM((layer, XR + YR, LANES), F32),
            pltpu.VMEM((2, slots, ROWS, LANES), F32),
            pltpu.VMEM((2, slots, ROWS, LANES), F32),
            pltpu.VMEM((2, layer, ROWS, LANES), F32),
            pltpu.VMEM((2, layer, ROWS, LANES), F32),
            pltpu.VMEM((layer, XR + YR, LANES), F32),
            pltpu.VMEM((2, slots, ROWS, LANES), F32),
            pltpu.VMEM((2, layer, ROWS, LANES), F32),
            pltpu.SemaphoreType.DMA((32,)),
            pltpu.SemaphoreType.DMA((32,)),
        ],
        compiler_params=pltpu.CompilerParams(
            collective_id=0, has_side_effects=True, vmem_limit_bytes=56 << 20
        ),
    )(
        levels,
        neighbours,
        relax_rates,
        diffusivity,
        stoichiometry,
        rows_of(populations),
        rows_of(scalars),
        rows_of(coarse_old),
        rows_of(coarse_new),
    )
    new_populations, new_scalars, ret_x, ret_y, ret_z = outs
    back = pl.pallas_call(
        means_kernel,
        out_shape=shape((slots, 6, 9, 64), F32),
        in_specs=[smem] + [vmem] * 3,
        out_specs=vmem,
        scratch_shapes=[pltpu.VMEM((slots // 2 * LANES, LANES), F32)],
    )(levels, ret_x, ret_y, ret_z)
    return (
        array_of(new_populations, slots, 27),
        array_of(new_scalars, slots, 9),
        back.reshape(slots, -1),
    )


def solution(mesh):
    in_specs = (
        P("blk", None, None),
        P("blk", None, None),
        P("blk", None, None),
        P("blk", None, None),
        P(),
        P("blk", None),
        P(),
        P(),
        P(),
    )
    out_specs = (P("blk", None, None), P("blk", None, None), P("blk", None))
    return jax.shard_map(local, mesh=mesh, in_specs=in_specs, out_specs=out_specs, check_vma=False)
```

```python
import jax
import jax.numpy as jnp
import numpy as np
from jax import lax
from jax.experimental import pallas as pl
from jax.experimental.pallas import tpu as pltpu
from jax.sharding import PartitionSpec as P

F32 = jnp.float32
MESH = pl.DeviceIdType.MESH
LANES = 128
ROWS = 32
HALF = 16
MOVERS = (
    (tuple(18 + p for p in range(9)), tuple(p for p in range(9))),
    (
        tuple(9 * (p // 3) + 6 + p % 3 for p in range(9)),
        tuple(9 * (p // 3) + p % 3 for p in range(9)),
    ),
    (tuple(3 * p + 2 for p in range(9)), tuple(3 * p for p in range(9))),
)
SCALAR_ROWS = (tuple(range(9)), tuple(range(9)))
XR = 40
POP_ROWS = 36 * 32
SCA_ROWS = 20 * 32
YR = 48


def lanes_of(rows):
    return lax.broadcasted_iota(jnp.int32, (rows, LANES), 1)


def flag(value, rows):
    return jnp.broadcast_to(value, (rows, LANES)) == 1


def roll(v, by, axis=1):
    size = v.shape[axis]
    by = by % size
    return v if by == 0 else pltpu.roll(v, by, axis)


def along(values, dim, func):
    out = [None] * 27
    step = (9, 3, 1)[dim]
    for base in range(27):
        if (base // step) % 3 == 0:
            a, b, c = func(values[base], values[base + step], values[base + 2 * step])
            out[base], out[base + step], out[base + 2 * step] = a, b, c
    return out


def to_moments(low, mid, high):
    both = low + high
    return both + 4.0 * mid, high - low, both


def from_moments(m0, m1, m2):
    return m2 - m1, m0 - 0.5 * m2, m1 + m2


def split(a):
    a0 = a.astype(jnp.bfloat16)
    rest = a - a0.astype(F32)
    a1 = rest.astype(jnp.bfloat16)
    return a0, a1, (rest - a1.astype(F32)).astype(jnp.bfloat16)


def product(parts, right):
    total = jnp.dot(parts[2], right, preferred_element_type=F32)
    total = total + jnp.dot(parts[1], right, preferred_element_type=F32)
    return total + jnp.dot(parts[0], right, preferred_element_type=F32)


def pack_x(load, put):
    for way in range(2):
        for half in range(2):
            put(way * 18 + half * 9, 9, load(0, way, None, half * HALF + (15 if way == 0 else 0)))


def pack_y(load, put):
    lane = lanes_of(HALF)
    last = None
    for way in range(2):
        slab = None
        for p in range(9):
            v = load(1, way, p, HALF if way == 0 else 0, HALF)
            source = 7 if way == 0 else 0
            slot = p if p < 8 else way
            v = roll(v, 16 * (slot - source))
            if p < 8:
                slab = v if slab is None else jnp.where(lane // 16 == slot, v, slab)
            else:
                last = v if last is None else jnp.where(lane // 16 == slot, v, last)
        put(way * HALF, HALF, slab)
    put(2 * HALF, HALF, last)


def pack_z(load, put):
    lane = lanes_of(ROWS) % 16
    for way in range(2):
        slab = None
        for p in range(9):
            v = roll(load(2, way, p, 0, ROWS), p - (15 if way == 0 else 0))
            slab = v if slab is None else jnp.where(lane == p, v, slab)
        put(way, slab)


def slab_face(ref, at, way, p, start):
    if p < 8:
        return roll(ref[at, pl.ds(way * HALF, HALF), :], start - 16 * p)
    return roll(ref[at, pl.ds(2 * HALF, HALF), :], start - 16 * way)


def kernel(
    levels,
    neighbours,
    rates,
    diffusivity,
    stoichiometry,
    pop,
    sca,
    old,
    new,
    out_pop,
    out_sca,
    ret_x,
    ret_y,
    ret_z,
    state,
    first,
    up0,
    up1,
    spec,
    spec2,
    res,
    slopes,
    bx_0,
    bx_1,
    by_0,
    by_1,
    bz_out_0,
    bz_out_1,
    bz_0,
    bz_1,
    sxy_0,
    sxy_1,
    sz_out_0,
    sz_out_1,
    sz_0,
    sz_1,
    rxy,
    rz_out,
    rz,
    send_sem,
    recv_sem,
):
    slots = neighbours.shape[0]
    devices = lax.axis_size("blk")
    me = lax.axis_index("blk")
    layers = devices // 2
    layer = me // 2
    core = me % 2
    partner = 2 * layer + 1 - core
    above = lax.rem(layer + 1, layers)
    below = lax.rem(layer + layers - 1, layers)
    mine = core * slots
    around = 2 * slots
    mesh_targets = (2 * above + core, 2 * below + core)

    barrier = pltpu.get_barrier_semaphore()
    for device in (partner,) + mesh_targets:
        pl.semaphore_signal(barrier, inc=1, device_id=(device,), device_id_type=MESH)

    counter = [0, 0]

    def send_partner(ref):
        s, r = counter[0], counter[1]
        counter[0] += 1
        counter[1] += 1
        part = ref.at[pl.ds(mine, slots)]
        copy = pltpu.make_async_remote_copy(
            src_ref=part,
            dst_ref=part,
            send_sem=send_sem.at[s],
            recv_sem=recv_sem.at[r],
            device_id=(partner,),
            device_id_type=MESH,
        )
        copy.start()
        other = ref.at[pl.ds(slots - mine, slots)]
        arrival = pltpu.make_async_remote_copy(
            src_ref=other,
            dst_ref=other,
            send_sem=send_sem.at[s],
            recv_sem=recv_sem.at[r],
            device_id=(partner,),
            device_id_type=MESH,
        )

        def wait():
            arrival.wait_recv()
            copy.wait_send()

        return wait

    def send_layers(source, target):
        copies = []
        for way in range(2):
            s, r = counter[0], counter[1]
            counter[0] += 1
            counter[1] += 1
            copy = pltpu.make_async_remote_copy(
                src_ref=source.at[way],
                dst_ref=target.at[way, pl.ds(mine, slots)],
                send_sem=send_sem.at[s],
                recv_sem=recv_sem.at[r],
                device_id=(mesh_targets[way],),
                device_id_type=MESH,
            )
            copy.start()
            copies.append(copy)

        def relay():
            waits = []
            for way in range(2):
                copies[way].wait_recv()
                waits.append(send_partner(target.at[way]))

            def wait():
                for way in range(2):
                    copies[way].wait_send()
                    waits[way]()

            return wait

        return relay

    def each_block(body):
        def wrapped(b, carry):
            body(b)
            return carry

        lax.fori_loop(0, slots, wrapped, 0)

    def fine_of(b):
        return levels[me * slots + b]

    def place(b, q):
        return lax.rem(neighbours[b, q], around)

    def native(i, half, b):
        return pl.ds(i * 2 * HALF * slots + half * slots + b, HALF, stride=2 * slots)

    def unpack_in(b):
        for half in range(2):
            for i in range(27):
                state[b, pl.ds(ROWS * i + half * HALF, HALF), :] = pop[native(i, half, b), :]
            for m in range(9):
                spec[b, pl.ds(ROWS * m + half * HALF, HALF), :] = sca[native(m, half, b), :]

    each_block(unpack_in)

    def spread_values(average):
        a = 0.5 * (old[...] + new[...]) if average else old[...]
        row = lax.broadcasted_iota(jnp.int32, (LANES, LANES), 0)
        col = lax.broadcasted_iota(jnp.int32, (LANES, LANES), 1)
        want = (col // 32) * 8 + (col % 16) // 2
        parts = split(a)
        for variant in range(4):
            at = variant // 2 * 64 + variant % 2 * 32
            pick = jnp.where(row == want + at, 1.0, 0.0).astype(jnp.bfloat16)
            res[variant, pl.ds(0, a.shape[0]), :] = product(parts, pick)

    def spread_rows(target, b, variant, chunk, xs):
        v = res[variant, pl.ds(chunk * slots + b, 27, stride=4 * slots), :]
        for x in xs:
            target[b, pl.ds(variant % 2 * HALF + x, 27, stride=ROWS), :] = v

    def spread_ends(target):
        def body(b):
            for half in range(2):
                spread_rows(target, b, half, 0, (0,))
                spread_rows(target, b, 2 + half, 3, (15,))

        each_block(body)

    def spread_all(target):
        def body(b):
            for variant in range(4):
                for chunk in range(4):
                    x = 2 * (2 * chunk + variant // 2)
                    spread_rows(target, b, variant, chunk, (x, x + 1))

        each_block(body)

    spread_values(False)
    spread_ends(up0)

    def population_load(b, spread):
        fine = fine_of(b)

        def load(dim, way, p, start, size=None):
            movers = MOVERS[dim][way]
            if p is None:
                at = pl.ds(ROWS * movers[0] + start, 9, stride=ROWS)
                return jnp.where(flag(fine, 9), state[b, at, :], spread[b, at, :])
            at = pl.ds(ROWS * movers[p] + start, size)
            return jnp.where(flag(fine, size), state[b, at, :], spread[b, at, :])

        return load

    def return_load(b):
        fine = fine_of(b)

        def load(dim, way, p, start, size=None):
            movers = MOVERS[dim][way]
            if p is None:
                at = pl.ds(ROWS * movers[0] + start, 9, stride=ROWS)
                rows = 9
            else:
                at = pl.ds(ROWS * movers[p] + start, size)
                rows = size
            return jnp.where(flag(fine, rows), 0.5 * first[b, at, :] + 0.5 * state[b, at, :], 0.0)

        return load

    def scalar_load(b, source):
        def load(dim, way, p, start, size=None):
            if p is None:
                return source[b, pl.ds(start, 9, stride=ROWS), :]
            return source[b, pl.ds(ROWS * p + start, size), :]

        return load

    def putter(ref, at, base=0):
        def put(start, size, value):
            ref[at, pl.ds(base + start, size), :] = value

        return put

    def putter_z(ref, b):
        def put(way, value):
            ref[way, b] = value

        return put

    def collide(keep):
        scale = [rates[k] * (3.375 / 216.0 * 2.0 ** sum(1 for d in (9, 3, 1) if (k // d) % 3)) for k in range(27)]

        def one(t, carry):
            b = t // 4
            base = pl.multiple_of((t % 4) * 8, 8)

            def at(i):
                return pl.ds(base + ROWS * i, 8)

            g = [state[b, at(i), :] for i in range(27)]
            m = along(along(along(g, 2, to_moments), 1, to_moments), 0, to_moments)
            rho = m[0]
            jx, jy, jz = m[9], m[3], m[1]
            unit = 1.0 / 216.0
            hx, hy, hz = jx * unit, jy * unit, jz * unit
            third = 1.0 / 3.0
            qx, qy, qz = jx * hx, jy * hy, jz * hz
            eq = [None] * 27
            eq[0] = rho
            eq[9], eq[3], eq[1] = jx, jy, jz
            rho3 = rho * third
            eq[18], eq[6], eq[2] = rho3 + qx, rho3 + qy, rho3 + qz
            xy, xz, yz = jx * hy, jx * hz, jy * hz
            eq[12], eq[10], eq[4] = xy, xz, yz
            jx3, jy3, jz3 = jx * third, jy * third, jz * third
            eq[21], eq[19] = jy3, jz3
            eq[15], eq[7] = jx3, jz3
            eq[11], eq[5] = jx3, jy3
            rho9 = rho3 * third
            qx3, qy3, qz3 = qx * third, qy * third, qz * third
            eq[24] = rho9 + qx3 + qy3
            eq[20] = rho9 + qx3 + qz3
            eq[8] = rho9 + qy3 + qz3
            eq[22], eq[16], eq[14] = yz * third, xz * third, xy * third
            eq[25], eq[23], eq[17] = jz3 * third, jy3 * third, jx3 * third
            eq[26] = (rho9 + qx3 + qy3 + qz3) * third
            delta = [
                scale[k] * (m[k] if eq[k] is None else m[k] - eq[k]) for k in range(27)
            ]
            back = along(along(along(delta, 0, from_moments), 1, from_moments), 2, from_moments)
            for i in range(27):
                post = state[b, at(i), :] - back[i]
                state[b, at(i), :] = post
                if keep:
                    first[b, at(i), :] = post
            return carry

        lax.fori_loop(0, slots * 4, one, 0)

    def shift_x(b):
        for p in range(9):
            for half in range(2):
                up = ROWS * MOVERS[0][0][p] + half * HALF
                down = ROWS * MOVERS[0][1][p] + half * HALF
                v = state[b, pl.ds(up, 15), :]
                w = state[b, pl.ds(down + 1, 15), :]
                state[b, pl.ds(up + 1, 15), :] = v
                state[b, pl.ds(down, 15), :] = w

    def enter_x(b, recv):
        low, high = place(b, 0), place(b, 1)
        for half in range(2):
            state[b, pl.ds(ROWS * 18 + half * HALF, 9, stride=ROWS), :] = recv[
                low, pl.ds(half * 9, 9), :
            ]
            state[b, pl.ds(half * HALF + 15, 9, stride=ROWS), :] = recv[
                high, pl.ds(18 + half * 9, 9), :
            ]

    def shift_y(b):
        lane = lanes_of(HALF)
        for p in range(9):
            even = pl.ds(ROWS * MOVERS[1][0][p], HALF)
            odd = pl.ds(ROWS * MOVERS[1][0][p] + HALF, HALF)
            e, o = roll(state[b, even, :], 16), roll(state[b, odd, :], 16)
            state[b, odd, :] = jnp.where(lane < 16, e, o)
            state[b, even, :] = e
            even = pl.ds(ROWS * MOVERS[1][1][p], HALF)
            odd = pl.ds(ROWS * MOVERS[1][1][p] + HALF, HALF)
            e, o = roll(state[b, even, :], -16), roll(state[b, odd, :], -16)
            state[b, even, :] = jnp.where(lane >= 112, o, e)
            state[b, odd, :] = o

    def enter_y(b, recv):
        lane = lanes_of(HALF)
        low, high = place(b, 2), place(b, 3)
        for p in range(9):
            at = pl.ds(ROWS * MOVERS[1][0][p], HALF)
            state[b, at, :] = jnp.where(lane < 16, slab_face(recv, low, 0, p, 0), state[b, at, :])
            at = pl.ds(ROWS * MOVERS[1][1][p] + HALF, HALF)
            state[b, at, :] = jnp.where(
                lane >= 112, slab_face(recv, high, 1, p, 112), state[b, at, :]
            )

    def shift_z(b):
        for p in range(9):
            at = pl.ds(ROWS * MOVERS[2][0][p], ROWS)
            state[b, at, :] = roll(state[b, at, :], 1)
            at = pl.ds(ROWS * MOVERS[2][1][p], ROWS)
            state[b, at, :] = roll(state[b, at, :], -1)

    def enter_z(b, recv):
        lane = lanes_of(ROWS) % 16
        low = recv[0, place(b, 4)]
        high = recv[1, place(b, 5)]
        for p in range(9):
            at = pl.ds(ROWS * MOVERS[2][0][p], ROWS)
            state[b, at, :] = jnp.where(lane == 0, roll(low, -p), state[b, at, :])
            at = pl.ds(ROWS * MOVERS[2][1][p], ROWS)
            state[b, at, :] = jnp.where(lane == 15, roll(high, 15 - p), state[b, at, :])

    def prepare(source, target, recv, recv_z):
        def body(b):
            row = lax.broadcasted_iota(jnp.int32, (HALF, LANES), 0)
            lane = lanes_of(HALF)
            near = lane % 16
            known = [flag(levels[neighbours[b, q]], HALF) for q in range(6)]
            spot = [place(b, q) for q in range(6)]
            e8 = [source[b, pl.ds(ROWS * 8 + h * HALF, HALF), :] for h in range(2)]
            burn = [
                source[b, pl.ds(h * HALF, HALF), :]
                * source[b, pl.ds(ROWS + h * HALF, HALF), :]
                * jnp.exp(4.0 * (e8[h] - 1.0))
                for h in range(2)
            ]
            for m in range(9):
                e = source[b, pl.ds(ROWS * m, HALF), :]
                o = source[b, pl.ds(ROWS * m + HALF, HALF), :]
                pair = (e, o)
                up_y, down_y = roll(e, -16), roll(o, -16)
                up_y = (
                    jnp.where(lane >= 112, down_y, up_y),
                    jnp.where(
                        lane >= 112,
                        jnp.where(known[3], slab_face(recv.at[:, pl.ds(XR, YR)], spot[3], 1, m, 112), o),
                        down_y,
                    ),
                )
                re, ro = roll(e, 16), roll(o, 16)
                down_y = (
                    jnp.where(
                        lane < 16,
                        jnp.where(known[2], slab_face(recv.at[:, pl.ds(XR, YR)], spot[2], 0, m, 0), e),
                        re,
                    ),
                    jnp.where(lane < 16, re, ro),
                )
                for half in range(2):
                    v = pair[half]
                    line = recv[spot[0], pl.ds(half * 9 + m, 1), :]
                    face = jnp.where(known[0], jnp.broadcast_to(line, v.shape), v)
                    down_x = jnp.where(row == 0, face, roll(v, 1, 0))
                    line = recv[spot[1], pl.ds(18 + half * 9 + m, 1), :]
                    face = jnp.where(known[1], jnp.broadcast_to(line, v.shape), v)
                    up_x = jnp.where(row == 15, face, roll(v, -1, 0))
                    face = roll(recv_z[0, spot[4], pl.ds(half * HALF, HALF), :], -m)
                    down_z = jnp.where(near == 0, jnp.where(known[4], face, v), roll(v, 1))
                    face = roll(recv_z[1, spot[5], pl.ds(half * HALF, HALF), :], 15 - m)
                    up_z = jnp.where(near == 15, jnp.where(known[5], face, v), roll(v, -1))
                    at = pl.ds(ROWS * m + half * HALF, HALF)
                    slopes[0, b, at, :] = 0.5 * (up_x - down_x)
                    slopes[1, b, at, :] = 0.5 * (up_y[half] - down_y[half])
                    slopes[2, b, at, :] = 0.5 * (up_z - down_z)
                    spread = (up_x + down_x) + (up_y[half] + down_y[half]) + (up_z + down_z) - 6.0 * v
                    target[b, at, :] = v + diffusivity[m] * spread + stoichiometry[m] * burn[half]

        each_block(body)

    def finish(target):
        def body(b):
            drift = []
            for half in range(2):

                def get(i):
                    return state[b, pl.ds(ROWS * i + half * HALF, HALF), :]

                g = [get(i) for i in range(27)]
                weighted = lambda a, c, f: (a + f) * (1.0 / 6.0) + c * (2.0 / 3.0)
                slope = lambda a, f: (f - a) * (1.0 / 6.0)
                zsum = [weighted(g[3 * k], g[3 * k + 1], g[3 * k + 2]) for k in range(9)]
                zdif = [slope(g[3 * k], g[3 * k + 2]) for k in range(9)]
                ysum = [weighted(zsum[3 * k], zsum[3 * k + 1], zsum[3 * k + 2]) for k in range(3)]
                ydif = [slope(zsum[3 * k], zsum[3 * k + 2]) for k in range(3)]
                zrow = [weighted(zdif[3 * k], zdif[3 * k + 1], zdif[3 * k + 2]) for k in range(3)]
                drift.append((slope(ysum[0], ysum[2]), weighted(*ydif), weighted(*zrow)))
            for m in range(9):
                for half in range(2):
                    at = pl.ds(ROWS * m + half * HALF, HALF)
                    jx, jy, jz = drift[half]
                    target[b, at, :] = target[b, at, :] - (
                        jx * slopes[0, b, at, :] + jy * slopes[1, b, at, :] + jz * slopes[2, b, at, :]
                    )

        each_block(body)

    pl.semaphore_wait(barrier, 3)
    last_wait = None
    for substep in range(2):
        spread = (up0, up1)[substep]
        source, target = (spec, spec2) if substep == 0 else (spec2, spec)
        cx, cy, cz_out, cz = ((bx_0, by_0, bz_out_0, bz_0), (bx_1, by_1, bz_out_1, bz_1))[substep]
        cs, cs_out, cs_z = ((sxy_0, sz_out_0, sz_0), (sxy_1, sz_out_1, sz_1))[substep]

        def pack_scalars(b):
            load = scalar_load(b, source)
            pack_x(load, putter(cs, mine + b))
            pack_y(load, putter(cs, mine + b, XR))
            pack_z(load, putter_z(cs_out, b))

        collide(substep == 0)
        each_block(lambda b: pack_x(population_load(b, spread), putter(cx, mine + b)))
        wait = send_partner(cx)
        each_block(pack_scalars)
        wait_s = send_partner(cs)
        relay_sz = send_layers(cs_out, cs_z)
        if substep == 1:

            def pack_return(b):
                load = return_load(b)
                pack_x(load, putter(rxy, mine + b))
                pack_y(load, putter(rxy, mine + b, XR))
                pack_z(load, putter_z(rz_out, b))

            each_block(pack_return)
        else:
            spread_all(up0)
        each_block(shift_x)
        wait()
        each_block(lambda b: enter_x(b, cx))
        each_block(lambda b: pack_y(population_load(b, spread), putter(cy, mine + b)))
        wait = send_partner(cy)
        if substep == 1:
            wait_r = send_partner(rxy)
        else:
            spread_values(True)
            spread_all(up1)
        each_block(shift_y)
        wait()
        each_block(lambda b: enter_y(b, cy))
        each_block(lambda b: pack_z(population_load(b, spread), putter_z(cz_out, b)))
        relay = send_layers(cz_out, cz)
        if substep == 1:
            relay_rz = send_layers(rz_out, rz)
        wait_sz = relay_sz()
        each_block(shift_z)
        wait_s()
        wait_sz()
        prepare(source, target, cs, cs_z)
        wait = relay()
        wait()
        if substep == 1:
            wait_rz = relay_rz()
        each_block(lambda b: enter_z(b, cz))
        finish(target)
    wait_r()
    wait_rz()

    def pack_out(b):
        fine = flag(fine_of(b), HALF)
        for half in range(2):
            for i in range(27):
                at = native(i, half, b)
                out_pop[at, :] = jnp.where(
                    fine, state[b, pl.ds(ROWS * i + half * HALF, HALF), :], pop[at, :]
                )
            for m in range(9):
                at = native(m, half, b)
                out_sca[at, :] = jnp.where(
                    fine, spec[b, pl.ds(ROWS * m + half * HALF, HALF), :], sca[at, :]
                )
        for way in range(2):
            at = place(b, way)
            ret_x[0, b, way, pl.ds(0, 9), :] = rxy[at, pl.ds(18 * way, 9), :]
            ret_x[1, b, way, pl.ds(0, 9), :] = rxy[at, pl.ds(18 * way + 9, 9), :]
            at = place(b, 2 + way)
            ret_y[b, way, pl.ds(0, HALF), :] = rxy[at, pl.ds(XR + HALF * way, HALF), :]
            ret_y[b, way, pl.ds(HALF, HALF), :] = rxy[at, pl.ds(XR + 2 * HALF, HALF), :]
            ret_z[b, way] = rz[way, place(b, 4 + way)]

    each_block(pack_out)


def means_kernel(levels, ret_x, ret_y, ret_z, out, turned):
    slots = out.shape[0]
    first = lax.axis_index("blk") * slots
    groups = slots // 2

    def mask(b, rows):
        return jnp.broadcast_to(levels[first + b], (rows, 64)) == 1

    def put(b, side, start, values):
        for p in range(values.shape[0]):
            at = (side * 9 + start + p) * 64
            out[pl.ds(b, 1), pl.ds(at, 64)] = values[p : p + 1]

    def grid(rows, columns):
        return tuple(lax.broadcasted_iota(jnp.int32, (rows, columns), d) for d in range(2))

    def pick(cond):
        return jnp.where(cond, 0.25, 0.0).astype(jnp.bfloat16)

    k, n = grid(LANES, 64)
    total = None
    for half in range(2):
        right = pick(n == half * 32 + (k // 32) * 8 + (k % 16) // 2)
        v = ret_x[half].reshape(slots * 2 * 16, LANES)
        part = product(split(v), right)
        total = part if total is None else total + part
    for b in range(slots):
        for way in range(2):
            v = total[(b * 2 + way) * 16 : (b * 2 + way) * 16 + 9]
            put(b, way, 0, jnp.where(mask(b, 9), 0.0, v))

    k, n = grid(LANES, 512)
    for g in range(groups):
        turned[pl.ds(g * LANES, LANES), :] = (
            ret_y[pl.ds(2 * g, 2)].reshape(LANES, LANES).T
        )
    total = None
    for z in range(8):
        left = (
            turned[pl.ds(2 * z, 8 * groups, stride=16), :]
            + turned[pl.ds(2 * z + 1, 8 * groups, stride=16), :]
        )
        right = pick(
            (k // 32 == (n % 256) // 64)
            & ((k % 32) // 16 == n // 256)
            & (n % 64 == ((k % 16) // 2) * 8 + z)
        )
        part = product(split(left), right)
        total = part if total is None else total + part
    for b in range(slots):
        for way in range(2):
            g, at = b // 2, (b % 2) * 2 + way
            v = total[g * 8 : g * 8 + 8, at * 64 : at * 64 + 64]
            w = total[g * 8 + way : g * 8 + way + 1, 256 + at * 64 : 256 + at * 64 + 64]
            put(b, 2 + way, 0, jnp.where(mask(b, 8), 0.0, v))
            put(b, 2 + way, 8, jnp.where(mask(b, 1), 0.0, w))

    k, n = grid(LANES, 256)
    total = [None] * groups
    for g in range(groups):
        turned[pl.ds(g * LANES, LANES), :] = (
            ret_z[pl.ds(2 * g, 2)].reshape(LANES, LANES).T
        )
    for y in range(4):
        right = pick(
            (k // 32 == n // 64)
            & (n % 64 == ((k % 16) // 2) * 8 + ((k % 32) // 16) * 4 + y)
        )
        for g in range(groups):
            base = g * LANES + 32 * y
            left = turned[pl.ds(base, 16), :] + turned[pl.ds(base + 16, 16), :]
            part = product(split(left), right)
            total[g] = part if total[g] is None else total[g] + part
    for b in range(slots):
        for way in range(2):
            at = (b % 2) * 2 + way
            v = total[b // 2][0:9, at * 64 : at * 64 + 64]
            put(b, 4 + way, 0, jnp.where(mask(b, 9), 0.0, v))


def rows_of(array):
    slots, k, cells = array.shape
    v = array.reshape(slots, k, cells // LANES, LANES).transpose(1, 2, 0, 3)
    return v.reshape(-1, LANES)


def array_of(rows, slots, k):
    v = rows.reshape(k, -1, slots, LANES).transpose(2, 0, 1, 3)
    return v.reshape(slots, k, -1)


def local(
    populations,
    scalars,
    coarse_old,
    coarse_new,
    levels,
    neighbours,
    relax_rates,
    diffusivity,
    stoichiometry,
):
    slots = populations.shape[0]
    vmem = pl.BlockSpec(memory_space=pltpu.VMEM)
    smem = pl.BlockSpec(memory_space=pltpu.SMEM)
    shape = jax.ShapeDtypeStruct
    layer = 2 * slots
    outs = pl.pallas_call(
        kernel,
        out_shape=(
            shape((slots * 27 * ROWS, LANES), F32),
            shape((slots * 9 * ROWS, LANES), F32),
            shape((2, slots, 2, 16, LANES), F32),
            shape((slots, 2, 32, LANES), F32),
            shape((slots, 2, 32, LANES), F32),
        ),
        in_specs=[smem] * 5 + [vmem] * 4,
        out_specs=[vmem] * 5,
        scratch_shapes=[
            pltpu.VMEM((slots, POP_ROWS, LANES), F32),
            pltpu.VMEM((slots, POP_ROWS, LANES), F32),
            pltpu.VMEM((slots, POP_ROWS, LANES), F32),
            pltpu.VMEM((slots, POP_ROWS, LANES), F32),
            pltpu.VMEM((slots, SCA_ROWS, LANES), F32),
            pltpu.VMEM((slots, SCA_ROWS, LANES), F32),
            pltpu.VMEM((4, slots * 4 * ROWS, LANES), F32),
            pltpu.VMEM((3, slots, 9 * ROWS, LANES), F32),
            pltpu.VMEM((layer + 1, XR, LANES), F32),
            pltpu.VMEM((layer + 1, XR, LANES), F32),
            pltpu.VMEM((layer, YR, LANES), F32),
            pltpu.VMEM((layer, YR, LANES), F32),
            pltpu.VMEM((2, slots, ROWS, LANES), F32),
            pltpu.VMEM((2, slots, ROWS, LANES), F32),
            pltpu.VMEM((2, layer, ROWS, LANES), F32),
            pltpu.VMEM((2, layer, ROWS, LANES), F32),
            pltpu.VMEM((layer, XR + YR, LANES), F32),
            pltpu.VMEM((layer, XR + YR, LANES), F32),
            pltpu.VMEM((2, slots, ROWS, LANES), F32),
            pltpu.VMEM((2, slots, ROWS, LANES), F32),
            pltpu.VMEM((2, layer, ROWS, LANES), F32),
            pltpu.VMEM((2, layer, ROWS, LANES), F32),
            pltpu.VMEM((layer, XR + YR, LANES), F32),
            pltpu.VMEM((2, slots, ROWS, LANES), F32),
            pltpu.VMEM((2, layer, ROWS, LANES), F32),
            pltpu.SemaphoreType.DMA((32,)),
            pltpu.SemaphoreType.DMA((32,)),
        ],
        compiler_params=pltpu.CompilerParams(
            collective_id=0, has_side_effects=True, vmem_limit_bytes=56 << 20
        ),
    )(
        levels,
        neighbours,
        relax_rates,
        diffusivity,
        stoichiometry,
        rows_of(populations),
        rows_of(scalars),
        rows_of(coarse_old),
        rows_of(coarse_new),
    )
    new_populations, new_scalars, ret_x, ret_y, ret_z = outs
    back = pl.pallas_call(
        means_kernel,
        out_shape=shape((slots, 6 * 9 * 64), F32),
        in_specs=[smem] + [vmem] * 3,
        out_specs=vmem,
        scratch_shapes=[pltpu.VMEM((slots // 2 * LANES, LANES), F32)],
    )(levels, ret_x, ret_y, ret_z)
    return (
        array_of(new_populations, slots, 27),
        array_of(new_scalars, slots, 9),
        back,
    )


def solution(mesh):
    in_specs = (
        P("blk", None, None),
        P("blk", None, None),
        P("blk", None, None),
        P("blk", None, None),
        P(),
        P("blk", None),
        P(),
        P(),
        P(),
    )
    out_specs = (P("blk", None, None), P("blk", None, None), P("blk", None))
    return jax.shard_map(local, mesh=mesh, in_specs=in_specs, out_specs=out_specs, check_vma=False)
```
